32 devices in a mesh: rows: 8 (over z, core), pairs: 4 (over y, x).
Axes of the slice: x: 2, y: 2, z: 4, core: 2. Of those that a mesh axis runs over, the one named last changes fastest.
Arguments:
- observed: float32 [12288, 2048], P('rows', 'pairs'), as said below
- estimate: float32 [12288, 2048], P('rows', 'pairs'), may hold values from -0.054126587 to 0.054126587
- mask: int32 [12288, 2048], P('rows', 'pairs'), may hold values from 0 to 1
- threshold: float32 [2048], P('pairs'), may hold values from 0.02 to 0.12
Outputs:
- regrouped: float32 [2048, 12288], P(('rows', 'pairs'))
The draws below stay inside these ranges and needn't reach their ends.
Inputs may be any that keep to these rules, and one draw needn't show every extreme that they name: observed has entries of order 12288^-1/2.
All inputs are finite; a program needn't handle non-finite values.
Results may differ from the reference program's by a relative error of at most 0.0003.
Values sent between devices are 32-bit elements; how exact they have to be, the bound alone decides.
A program may use at most 128 MiB of HBM per device.

```python
import jax
import jax.numpy as jnp
from jax import lax

BW = 128
ROUNDS = 4
NS_STEPS = 3
ROWS = 12288
COLS = 2048
N_PAIRS = 4


def draw_observed(key, part):
    key_noise = jax.random.fold_in(key, 11)
    key_shared = jax.random.fold_in(key, 12)
    key_scale = jax.random.fold_in(key, 13)
    groups = COLS // (2 * BW)
    noise = jax.random.normal(key_noise, (ROWS, COLS), jnp.float32)
    shared = jax.random.normal(key_shared, (ROWS, groups, 1, BW), jnp.float32)
    colscale = jax.random.uniform(key_scale, (COLS,), jnp.float32, 0.6, 1.6)
    shared = jnp.broadcast_to(shared, (ROWS, groups, 2, BW)).reshape(ROWS, COLS)
    values = (noise + 0.7 * shared) * colscale[None, :] / jnp.sqrt(1.49 * ROWS)
    return values.astype(jnp.float32)


def touch_ends(array, rng, low, high):
    shape = array.shape
    place = [jax.random.randint(jax.random.fold_in(rng, axis), (), 0, shape[axis]) for axis in range(len(shape))]
    array = array.at[tuple(place)].set(low)
    longest = shape.index(max(shape))
    place[longest] = (place[longest] + 1) % shape[longest]
    return array.at[tuple(place)].set(high)


def block_levels(key, shape, shards, least, top_value):
    level = 1.0
    for dim, blocks in shards:
        steps = jax.random.uniform(jax.random.fold_in(jax.random.fold_in(key, 6), dim), (blocks,), jnp.float32, least / len(shards), top_value / len(shards))
        level = level * jnp.repeat(jnp.exp(steps), shape[dim] // blocks).reshape((-1,) + (1,) * (len(shape) - 1 - dim))
    return level


def centred(stream_key, extent, scale, limit, split=(), kind=jnp.bfloat16):
    drawn = scale * jax.random.normal(stream_key, extent, jnp.float32)
    if split:
        drawn = drawn * block_levels(stream_key, extent, split, -0.22, 0.18)
    return jnp.clip(drawn, -limit, limit).astype(kind)


def setup_inputs(seed: int = 0) -> dict:
    key_list = jax.random.split(jax.random.key(seed), 5)
    observed = draw_observed(jax.random.fold_in(key_list[4], 71), 0)
    estimate = centred(key_list[1], (ROWS, COLS), (ROWS ** -0.5), 0.054126587, ((0, 8), (1, 4)), jnp.float32)
    mask = touch_ends(jax.random.randint(key_list[2], (ROWS, COLS), 0, 2), jax.random.fold_in(key_list[2], 1), 0, 1).astype(jnp.int32)
    threshold = jnp.clip(0.02 + 0.09999999776482582 * jax.random.uniform(key_list[3], (COLS,), jnp.float32) ** block_levels(key_list[3], (COLS,), ((0, 4),), -0.2, 0.2), 0.02, 0.12)
    return {"observed": observed, "estimate": estimate, "mask": mask, "threshold": threshold}


HI = lax.Precision.HIGHEST

def whitening_of(gram):
    width = gram.shape[-1]
    eye = jnp.eye(width, dtype=jnp.float32)
    dsum = jnp.diagonal(gram, axis1=-2, axis2=-1) + 1e-06
    inv_root = 1.0 / jnp.sqrt(dsum)
    normed = gram * inv_root[..., :, None] * inv_root[..., None, :]
    fro = jnp.sqrt(lax.optimization_barrier(jnp.sum(normed * normed, axis=(-2, -1))))
    ymat = normed / fro[..., None, None]
    zmat = jnp.broadcast_to(eye, normed.shape)
    for step in range(NS_STEPS):
        tmat = 1.5 * eye - 0.5 * jnp.einsum('...ij,...jk->...ik', zmat, ymat, precision=HI)
        ymat = jnp.einsum('...ij,...jk->...ik', ymat, tmat, precision=HI)
        zmat = jnp.einsum('...ij,...jk->...ik', tmat, zmat, precision=HI)
    return inv_root[..., :, None] * zmat * jnp.sqrt(dsum)[..., None, :] / jnp.sqrt(fro)[..., None, None]

def reference(observed, estimate, mask, threshold):
    filled = jnp.where(mask == 1, observed, estimate)
    total = filled.shape[0]
    groups = N_PAIRS
    blocks = filled.reshape(total, groups, 4, BW)
    for round_index in range(ROUNDS):
        pairs = blocks.reshape(total, groups, 2, 2 * BW)
        gram = jnp.einsum('rdpi,rdpj->dpij', pairs, pairs, precision=HI)
        whitening = whitening_of(gram)
        pairs = jnp.einsum('rdpi,dpij->rdpj', pairs, whitening, precision=HI)
        blocks = pairs.reshape(total, groups, 4, BW)
        if round_index + 1 < ROUNDS:
            first = blocks[:, :, 1]
            third = blocks[:, :, 3]
            blocks = jnp.stack([blocks[:, :, 0], jnp.roll(third, 1, axis=1), blocks[:, :, 2], first], axis=2)
    filled = blocks.reshape(total, groups * 4 * BW)
    col_norm = jnp.sqrt(lax.optimization_barrier(jnp.sum(filled * filled, axis=0)) + 1e-06)
    factor = jnp.maximum(col_norm - threshold, 0.0) / col_norm
    shrunk = filled * factor[None, :]
    return shrunk.reshape(total, groups, 4 * BW).transpose(2, 1, 0).reshape(groups * 4 * BW, total)
```

```python
import functools

import jax
import jax.numpy as jnp
from jax import lax
from jax.experimental import pallas as pl
from jax.experimental.pallas import tpu as pltpu
from jax.sharding import PartitionSpec as P

MESH = pl.DeviceIdType.MESH
F32 = jnp.float32
BF16 = jnp.bfloat16
NN = (((1,), (0,)), ((), ()))
NT = (((1,), (1,)), ((), ()))


def split(a):
    high = a.astype(BF16)
    return high, (a - high.astype(F32)).astype(BF16)


def dot_parts(a, b, dims):
    def one(x, y):
        return lax.dot_general(x, y, dims, preferred_element_type=F32)

    return one(a[0], b[0]) + (one(a[0], b[1]) + one(a[1], b[0]))


def dot3(a, b, dims=NN):
    return dot_parts(split(a), split(b), dims)


def whitening_t(gram):
    width = gram.shape[0]
    eye = (
        lax.broadcasted_iota(jnp.int32, (width, width), 0)
        == lax.broadcasted_iota(jnp.int32, (width, width), 1)
    ).astype(F32)
    on_diag = gram * eye
    d_col = jnp.sum(on_diag, axis=1, keepdims=True) + 1e-06
    d_row = jnp.sum(on_diag, axis=0, keepdims=True) + 1e-06
    i_col = 1.0 / jnp.sqrt(d_col)
    i_row = 1.0 / jnp.sqrt(d_row)
    normed = gram * i_col * i_row
    sq = jnp.sum(jnp.sum(normed * normed, axis=1, keepdims=True), axis=0, keepdims=True)
    fro = jnp.sqrt(sq)
    y = normed / fro
    t = 1.5 * eye - 0.5 * y
    z = t
    y = dot3(y, t)
    t = 1.5 * eye - 0.5 * dot3(z, y)
    y, z = dot3(y, t), dot3(t, z)
    t = 1.5 * eye - 0.5 * dot3(z, y)
    z = dot3(t, z)
    return jnp.sqrt(d_col) * z * i_row / jnp.sqrt(fro)


def join(ss, sm, mm):
    top = jnp.concatenate([ss, sm], axis=1)
    low = jnp.concatenate([sm.T, mm], axis=1)
    return jnp.concatenate([top, low], axis=0)


def square(width):
    shape = (width, width)
    return lax.broadcasted_iota(jnp.int32, shape, 0), lax.broadcasted_iota(jnp.int32, shape, 1)


def pack(gram, n_own):
    bw = gram.shape[0] // 2
    ss, sm, mm = gram[:bw, :bw], gram[:bw, bw:], gram[bw:, bw:]
    r, c = square(bw)
    diag = jnp.sum(jnp.where(r == c, mm, 0.0), axis=0, keepdims=True)
    return [jnp.where(r <= c, ss, mm), sm, jnp.broadcast_to(diag, (8 * n_own, bw))]


def unpack(packed):
    bw = packed.shape[1]
    both, sm, diag = packed[:bw], packed[bw : 2 * bw], packed[2 * bw : 2 * bw + 1]
    r, c = square(bw)
    flip = both.T
    mm = jnp.where(r == c, diag, jnp.where(r > c, both, flip))
    return join(jnp.where(r <= c, both, flip), sm, mm)


def owners(n_rows):
    return (n_rows // 4, n_rows // 2) if n_rows % 4 == 0 else (0, n_rows)


def sizes_of(bw, n_own):
    return [2 * bw + 8 * n_own] * 2 + [bw] * 6


def kernel(
    n_rows, n_pairs, step, early,
    obs_ref, est_ref, mask_ref, thr_ref, out_ref,
    obs_in, est_in, mask_in, x, keep, pay, land, res, gmm_out, gmm_in, last_hi, last_lo, send, far, onward,
    rs_s, rs_r, ag_s, ag_r, pm_s, pm_r, pg_s, pg_r, out_s, out_r, own_sem, in_sem, far_s, far_r,
):
    me = lax.axis_index("rows")
    group = lax.axis_index("pairs")
    n = n_rows * n_pairs
    bw = x.shape[2]
    rows = x.shape[3]
    chunks = rows // step
    each = send.shape[1]
    count = n // 2
    side = me // (n_rows // 2)
    partner = lax.rem(me + n_rows // 2, n_rows)
    partner_k = partner * n_pairs + group
    first, n_own = owners(n_rows)
    owner = (me >= first) & (me < first + n_own)
    sizes = sizes_of(bw, n_own)

    def fetches(half):
        cols = pl.ds(half * 2 * bw, 2 * bw)
        pairs = ((obs_ref, obs_in), (est_ref, est_in), (mask_ref, mask_in))
        return [
            pltpu.make_async_copy(src.at[:, cols], dst.at[:, cols], in_sem.at[half, i])
            for i, (src, dst) in enumerate(pairs)
        ]

    for half in (1, 0):
        for fetch in fetches(half):
            fetch.start()

    barrier = pltpu.get_barrier_semaphore()
    my_k = me * n_pairs + group

    def greet(i, carry):
        k = lax.rem(my_k + i, n)
        pl.semaphore_signal(
            barrier, inc=1, device_id=(k // n_pairs, lax.rem(k, n_pairs)), device_id_type=MESH
        )
        return carry

    lax.fori_loop(1, n, greet, 0)

    def fill(half):
        for fetch in fetches(half):
            fetch.wait()
        for slot in (2 * half, 2 * half + 1):
            cols = slice(slot * bw, (slot + 1) * bw)
            for c in range(chunks):
                part = slice(c * step, (c + 1) * step)
                filled = jnp.where(mask_in[part, cols] == 1, obs_in[part, cols], est_in[part, cols])
                x[0, slot, :, part] = filled.T

    def full_gram(s, m):
        total = jnp.zeros((2 * bw, 2 * bw), F32)
        for c in range(chunks):
            part = slice(c * step, (c + 1) * step)
            both = split(jnp.concatenate([s[:, part], m[:, part]], axis=0))
            total += dot_parts(both, both, NT)
        return total

    def cross_gram(s, m):
        total = jnp.zeros((2 * bw, 2 * bw), F32)
        for c in range(chunks):
            part = slice(c * step, (c + 1) * step)
            s_parts = jnp.concatenate(split(s[:, part]), axis=0)
            m_parts = jnp.concatenate(split(m[:, part]), axis=0)
            total += lax.dot_general(s_parts, m_parts, NT, preferred_element_type=F32)
        return total[:bw, :bw] + (total[:bw, bw:] + total[bw:, :bw])

    def place(b):
        return sum(sizes[:b]), sum(sizes[:b]) // n_own, sizes[b] // n_own

    def own(b, q):
        base, _, piece = place(b)
        return pl.ds(pl.multiple_of(base + q * piece, 8), piece)

    def fill_pay(b, blocks):
        at = place(b)[0]
        for block in blocks:
            pay[at : at + block.shape[0], :] = block
            at += block.shape[0]

    def reduce_start(b, blocks=()):
        _, lbase, piece = place(b)
        fill_pay(b, blocks)
        if b == 0:
            pl.semaphore_wait(barrier, n - 1)

        def scatter(i, carry):
            q = lax.rem(me + i, n_own)
            peer = first + q

            @pl.when(peer != me)
            def _():
                pltpu.make_async_remote_copy(
                    pay.at[own(b, q)], land.at[lax.rem(me + n_rows - peer, n_rows), pl.ds(lbase, piece)],
                    rs_s.at[b], rs_r.at[b], device_id=(peer, group), device_id_type=MESH,
                ).start()

            return carry

        lax.fori_loop(0, n_own, scatter, 0)

    def wait_pieces(b, some, sem):
        _, lbase, piece = place(b)
        ref = land.at[pl.ds(0, some), pl.ds(lbase, piece)]
        pltpu.make_async_copy(ref, ref, sem).wait()

    def reduce_mid(b):
        _, lbase, piece = place(b)

        @pl.when(owner)
        def _():
            wait_pieces(b, n_rows - 1, rs_r.at[b])
            mine = own(b, me - first)
            total = pay[mine, :]
            for off in range(1, n_rows):
                total += land[off, lbase : lbase + piece, :]
            res[mine, :] = total

            def gather(off, carry):
                peer = lax.rem(me + off, n_rows)
                pltpu.make_async_remote_copy(
                    res.at[mine], res.at[mine],
                    ag_s.at[b], ag_r.at[b], device_id=(peer, group), device_id_type=MESH,
                ).start()
                return carry

            lax.fori_loop(1, n_rows, gather, 0)

    def pieces_to_owners(b, sem):
        @pl.when(owner)
        def _():
            wait_pieces(b, n_own - 1, sem)

        @pl.when(jnp.logical_not(owner))
        def _():
            wait_pieces(b, n_own, sem)

    def reduce_end(b):
        base, _, _ = place(b)
        pieces_to_owners(b, ag_r.at[b])
        return res[base : base + sizes[b], :]

    def settle(b):
        pieces_to_owners(b, rs_s.at[b])

        @pl.when(owner)
        def _():
            wait_pieces(b, n_rows - 1, ag_s.at[b])

    def put(v_parts, s, m, write, start=0, stop=None):
        stop = s.shape[1] if stop is None else stop
        for at in range(start, stop, step):
            part = slice(at, min(at + step, stop))
            both = split(jnp.concatenate([s[:, part], m[:, part]], axis=0))
            write(part, dot_parts(v_parts, both, NN))

    def into(ref):
        def write(part, value):
            ref[:, part] = value
        return write

    right = lax.rem(group + 1, n_pairs)

    def pass_copy(src, dst, send_sem, recv_sem):
        return pltpu.make_async_remote_copy(
            src, dst, send_sem, recv_sem, device_id=(me, right), device_id_type=MESH
        )

    def put_and_pass(i, v_half, s, m):
        def write(part, value):
            keep[i, :, part] = value
            pass_copy(
                keep.at[i, :, part], x.at[i + 1, 1, :, part], pm_s.at[i], pm_r.at[i]
            ).start()

        put(split(v_half), s, m, write)

    def pass_gram(i, gmm):
        gmm_out[i] = gmm
        small = pass_copy(gmm_out.at[i], gmm_in.at[i], pg_s.at[i], pg_r.at[i])
        small.start()
        return pass_copy(keep.at[i], x.at[i + 1, 1], pm_s.at[i], pm_r.at[i]), small

    def new_grams(v, gram):
        vg = dot3(v, gram)
        return dot3(vg[:bw], v[:bw], NT), dot3(vg[bw:], v[bw:], NT)

    n_early = early // 128

    def far_copy(half, j, at, size):
        return pltpu.make_async_remote_copy(
            x.at[3, 2 * half + j, :, pl.ds(at, size)], far.at[j, :, pl.ds(at, size)],
            far_s.at[j], far_r.at[j], device_id=(partner, group), device_id_type=MESH,
        )

    shipped = [0, 0]

    def ship(half, some):
        for i in range(shipped[half], min(shipped[half] + some, 2 * n_early)):
            @pl.when(side != half)
            def _():
                far_copy(half, i // n_early, i % n_early * 128, 128).start()
        shipped[half] += some

    def scale_last(half, v, gram):
        vg = dot3(v, gram)
        squares = jnp.sum(vg * v, axis=1, keepdims=True)
        norm = jnp.sqrt(squares + 1e-06)
        eye = (
            lax.broadcasted_iota(jnp.int32, gram.shape, 0)
            == lax.broadcasted_iota(jnp.int32, gram.shape, 1)
        )
        level = thr_ref[:, 2 * half * bw : 2 * (half + 1) * bw]
        level = jnp.sum(jnp.where(eye, level, 0.0), axis=1, keepdims=True)
        last_hi[half], last_lo[half] = split((jnp.maximum(norm - level, 0.0) / norm) * v)

    per_block = bw // each

    def finish(half, target, base, s, m, start, stop):
        for j in range(2):
            def write(part, value):
                for i in range(per_block):
                    target[base + j * per_block + i, :, part] = value[i * each : (i + 1) * each]

            cut = slice(j * bw, (j + 1) * bw)
            put((last_hi[half, cut], last_lo[half, cut]), s, m, write, start, stop)

    def to(k):
        return dict(device_id=(k // n_pairs, lax.rem(k, n_pairs)), device_id_type=MESH)

    def deliver(half, same):
        def go(i, carry):
            k = half * count + lax.rem(my_k + i, count)
            if not same:
                pltpu.make_async_remote_copy(
                    send.at[k, :, early:], out_ref.at[my_k, :, early:], out_s.at[1], out_r.at[1], **to(k)
                ).start()
                return carry

            @pl.when(k != my_k)
            def _():
                pltpu.make_async_remote_copy(
                    send.at[k], out_ref.at[my_k], out_s.at[0], out_r.at[0], **to(k)
                ).start()

            @pl.when(k == my_k)
            def _():
                pltpu.make_async_copy(send.at[k], out_ref.at[my_k], own_sem.at[0]).start()

            return carry

        lax.fori_loop(0, count, go, 0)

    def deliver_onward():
        def go(i, carry):
            at = lax.rem(my_k + i, count)
            k = side * count + at
            spot = out_ref.at[partner_k, :, :early]

            @pl.when(k != my_k)
            def _():
                pltpu.make_async_remote_copy(
                    onward.at[at], spot, out_s.at[2], out_r.at[2], **to(k)
                ).start()

            @pl.when(k == my_k)
            def _():
                pltpu.make_async_copy(onward.at[at], spot, own_sem.at[1]).start()

            return carry

        lax.fori_loop(0, count, go, 0)

    fill(1)
    reduce_start(0, pack(full_gram(x.at[0, 2], x.at[0, 3]), n_own))
    fill(0)
    fill_pay(1, pack(full_gram(x.at[0, 0], x.at[0, 1]), n_own))
    reduce_mid(0)
    reduce_start(1)
    gb = unpack(reduce_end(0))
    vb = whitening_t(gb)
    put_and_pass(0, vb[bw:], x.at[0, 2], x.at[0, 3])
    reduce_mid(1)
    bs, bm = new_grams(vb, gb)
    sent = [pass_gram(0, bm)]
    put(split(vb[:bw]), x.at[0, 2], x.at[0, 3], into(x.at[1, 2]))
    ga = unpack(reduce_end(1))
    va = whitening_t(ga)
    put(split(va[bw:]), x.at[0, 0], x.at[0, 1], into(x.at[1, 3]))

    reduce_start(2, [cross_gram(x.at[1, 2], x.at[1, 3])])
    put(split(va[:bw]), x.at[0, 0], x.at[0, 1], into(x.at[1, 0]))
    as_, am = new_grams(va, ga)
    reduce_mid(2)
    gb = join(bs, reduce_end(2), am)
    vb = whitening_t(gb)
    put_and_pass(1, vb[bw:], x.at[1, 2], x.at[1, 3])
    for c in sent[0]:
        c.wait_recv()
    reduce_start(3, [cross_gram(x.at[1, 0], x.at[1, 1])])
    bs, bm = new_grams(vb, gb)
    sent.append(pass_gram(1, bm))
    put(split(vb[:bw]), x.at[1, 2], x.at[1, 3], into(x.at[2, 2]))
    reduce_mid(3)
    ga = join(as_, reduce_end(3), gmm_in[0])
    va = whitening_t(ga)
    put(split(va[bw:]), x.at[1, 0], x.at[1, 1], into(x.at[2, 3]))

    reduce_start(4, [cross_gram(x.at[2, 2], x.at[2, 3])])
    put(split(va[:bw]), x.at[1, 0], x.at[1, 1], into(x.at[2, 0]))
    as_, am = new_grams(va, ga)
    reduce_mid(4)
    gb = join(bs, reduce_end(4), am)
    for c in sent[1]:
        c.wait_recv()
    reduce_start(5, [cross_gram(x.at[2, 0], x.at[2, 1])])
    vb = whitening_t(gb)
    put_and_pass(2, vb[bw:], x.at[2, 2], x.at[2, 3])
    bs, bm = new_grams(vb, gb)
    sent.append(pass_gram(2, bm))
    put(split(vb[:bw]), x.at[2, 2], x.at[2, 3], into(x.at[3, 2]))
    ship(1, SHIP[0])
    reduce_mid(5)
    ship(1, SHIP[1])
    ga = join(as_, reduce_end(5), gmm_in[1])
    va = whitening_t(ga)
    put(split(va[bw:]), x.at[2, 0], x.at[2, 1], into(x.at[3, 3]))

    reduce_start(6, [cross_gram(x.at[3, 2], x.at[3, 3])])
    ship(1, SHIP[2])
    put(split(va[:bw]), x.at[2, 0], x.at[2, 1], into(x.at[3, 0]))
    ship(0, SHIP[3])
    as_, am = new_grams(va, ga)
    reduce_mid(6)
    ship(1, SHIP[4])
    ship(0, min(SHIP[5], n_early - SHIP[3]))
    for c in sent[2]:
        c.wait_recv()
    reduce_start(7, [cross_gram(x.at[3, 0], x.at[3, 1])])
    ship(1, SHIP[6])
    ship(0, SHIP[7])
    gb = join(bs, reduce_end(6), am)
    scale_last(1, whitening_t(gb), gb)
    reduce_mid(7)
    ship(1, 2 * n_early)
    ship(0, 2 * n_early)
    ga = join(as_, reduce_end(7), gmm_in[2])
    scale_last(0, whitening_t(ga), ga)

    for half in (1, 0):
        @pl.when(side != half)
        def _():
            finish(half, send, half * count, x.at[3, 2 * half], x.at[3, 2 * half + 1], early, rows)
            deliver(half, False)

    for half in (1, 0):
        @pl.when(side == half)
        def _():
            finish(half, send, half * count, x.at[3, 2 * half], x.at[3, 2 * half + 1], 0, rows)
            deliver(half, True)
            for j in range(2):
                far_copy(half, j, 0, early).wait_recv()
            finish(half, onward, 0, far.at[0], far.at[1], 0, early)
            deliver_onward()

    for b in range(len(sizes)):
        settle(b)
    for pair in sent:
        for c in pair:
            c.wait_send()
    for j in range(2):
        far_copy(0, j, 0, early).wait_send()
    pltpu.make_async_copy(send.at[0], out_ref.at[my_k], own_sem.at[0]).wait()
    pltpu.make_async_copy(onward.at[0], out_ref.at[my_k, :, :early], own_sem.at[1]).wait()
    for ref, sems in ((send, out_s), (out_ref, out_r)):
        for i, some in enumerate((
            ref.at[pl.ds(0, count - 1)],
            ref.at[pl.ds(0, count), :, early:],
            ref.at[pl.ds(0, count - 1), :, :early],
        )):
            pltpu.make_async_copy(some, some, sems.at[i]).wait()


def interleave(in_ref, out_ref):
    n_pairs, each, _ = in_ref.shape
    for i in range(each):
        out_ref[i * n_pairs : (i + 1) * n_pairs, :] = in_ref[:, i, :]


SHIP = (1, 1, 2, 1, 1, 3, 2, 1)


def on_device(observed, estimate, mask, threshold):
    n_rows = lax.axis_size("rows")
    n_pairs = lax.axis_size("pairs")
    rows, width = observed.shape
    bw = width // 4
    n = n_rows * n_pairs
    each = width // n
    step = 512 if rows % 512 == 0 else rows
    early = rows * 5 // 12 // 128 * 128 or rows
    n_own = owners(n_rows)[1]
    sizes = sizes_of(bw, n_own)
    total = sum(sizes)
    vmem = pl.BlockSpec(memory_space=pltpu.VMEM)
    dma = pltpu.SemaphoreType.DMA
    nb = len(sizes)
    landed = pl.pallas_call(
        functools.partial(kernel, n_rows, n_pairs, step, early),
        out_shape=jax.ShapeDtypeStruct((n, each, rows), F32),
        in_specs=[pl.BlockSpec(memory_space=pl.ANY)] * 3 + [vmem],
        out_specs=pl.BlockSpec(memory_space=pl.ANY),
        scratch_shapes=[
            pltpu.VMEM((rows, width), F32),
            pltpu.VMEM((rows, width), F32),
            pltpu.VMEM((rows, width), jnp.int32),
            pltpu.VMEM((4, 4, bw, rows), F32),
            pltpu.VMEM((3, bw, rows), F32),
            pltpu.VMEM((total, bw), F32),
            pltpu.VMEM((n_rows, total // n_own, bw), F32),
            pltpu.VMEM((total, bw), F32),
            pltpu.VMEM((3, bw, bw), F32),
            pltpu.VMEM((3, bw, bw), F32),
            pltpu.VMEM((2, 2 * bw, 2 * bw), BF16),
            pltpu.VMEM((2, 2 * bw, 2 * bw), BF16),
            pltpu.VMEM((n, each, rows), F32),
            pltpu.VMEM((2, bw, early), F32),
            pltpu.VMEM((n // 2, each, early), F32),
            dma((nb,)), dma((nb,)), dma((nb,)), dma((nb,)),
            dma((3,)), dma((3,)), dma((3,)), dma((3,)),
            dma((3,)), dma((3,)), dma((2,)), dma((2, 3)), dma((2,)), dma((2,)),
        ],
        compiler_params=pltpu.CompilerParams(
            collective_id=0, has_side_effects=True, vmem_limit_bytes=60 * 1024 * 1024
        ),
    )(observed, estimate, mask, threshold.reshape(1, width))
    landed = landed.reshape(n_rows, n_pairs, each, rows)
    return pl.pallas_call(
        interleave,
        grid=(n_rows,),
        out_shape=jax.ShapeDtypeStruct((each * n_pairs, n_rows * rows), F32),
        in_specs=[pl.BlockSpec((None, n_pairs, each, rows), lambda r: (r, 0, 0, 0))],
        out_specs=pl.BlockSpec((each * n_pairs, rows), lambda r: (0, r)),
    )(landed)


def solution(mesh):
    placed = (P("rows", "pairs"), P("rows", "pairs"), P("rows", "pairs"), P("pairs"))
    return jax.shard_map(
        on_device, mesh=mesh, in_specs=placed, out_specs=P(("rows", "pairs"), None), check_vma=False
    )
```

```python
import functools

import jax
import jax.numpy as jnp
from jax import lax
from jax.experimental import pallas as pl
from jax.experimental.pallas import tpu as pltpu
from jax.sharding import PartitionSpec as P

MESH = pl.DeviceIdType.MESH
F32 = jnp.float32
BF16 = jnp.bfloat16
NN = (((1,), (0,)), ((), ()))
NT = (((1,), (1,)), ((), ()))


def split(a):
    high = a.astype(BF16)
    return high, (a - high.astype(F32)).astype(BF16)


def dot_parts(a, b, dims):
    def one(x, y):
        return lax.dot_general(x, y, dims, preferred_element_type=F32)

    return one(a[0], b[0]) + (one(a[0], b[1]) + one(a[1], b[0]))


def dot3(a, b, dims=NN):
    return dot_parts(split(a), split(b), dims)


def whitening_t(gram):
    width = gram.shape[0]
    eye = (
        lax.broadcasted_iota(jnp.int32, (width, width), 0)
        == lax.broadcasted_iota(jnp.int32, (width, width), 1)
    ).astype(F32)
    on_diag = gram * eye
    d_col = jnp.sum(on_diag, axis=1, keepdims=True) + 1e-06
    d_row = jnp.sum(on_diag, axis=0, keepdims=True) + 1e-06
    i_col = 1.0 / jnp.sqrt(d_col)
    i_row = 1.0 / jnp.sqrt(d_row)
    normed = gram * i_col * i_row
    sq = jnp.sum(jnp.sum(normed * normed, axis=1, keepdims=True), axis=0, keepdims=True)
    fro = jnp.sqrt(sq)
    y = normed / fro
    t = 1.5 * eye - 0.5 * y
    z = t
    y = dot3(y, t)
    t = 1.5 * eye - 0.5 * dot3(z, y)
    y, z = dot3(y, t), dot3(t, z)
    t = 1.5 * eye - 0.5 * dot3(z, y)
    z = dot3(t, z)
    return jnp.sqrt(d_col) * z * i_row / jnp.sqrt(fro)


def join(ss, sm, mm):
    top = jnp.concatenate([ss, sm], axis=1)
    low = jnp.concatenate([sm.T, mm], axis=1)
    return jnp.concatenate([top, low], axis=0)


def square(width):
    shape = (width, width)
    return lax.broadcasted_iota(jnp.int32, shape, 0), lax.broadcasted_iota(jnp.int32, shape, 1)


def pack(gram, n_own):
    bw = gram.shape[0] // 2
    ss, sm, mm = gram[:bw, :bw], gram[:bw, bw:], gram[bw:, bw:]
    r, c = square(bw)
    diag = jnp.sum(jnp.where(r == c, mm, 0.0), axis=0, keepdims=True)
    return [jnp.where(r <= c, ss, mm), sm, jnp.broadcast_to(diag, (8 * n_own, bw))]


def unpack(packed):
    bw = packed.shape[1]
    both, sm, diag = packed[:bw], packed[bw : 2 * bw], packed[2 * bw : 2 * bw + 1]
    r, c = square(bw)
    flip = both.T
    mm = jnp.where(r == c, diag, jnp.where(r > c, both, flip))
    return join(jnp.where(r <= c, both, flip), sm, mm)


def owners(n_rows):
    return (n_rows // 4, n_rows // 2) if n_rows % 4 == 0 else (0, n_rows)


def sizes_of(bw, n_own):
    return [2 * bw + 8 * n_own] * 2 + [bw] * 6


def kernel(
    n_rows, n_pairs, step, early, ahead,
    obs_ref, est_ref, mask_ref, thr_ref, out_ref,
    obs_in, est_in, mask_in, x, keep, pay, land, res, gmm_out, gmm_in, last_hi, last_lo, send, far, onward, raw, v_out, v_in,
    rs_s, rs_r, ag_s, ag_r, pm_s, pm_r, pg_s, pg_r, out_s, out_r, own_sem, in_sem, far_s, far_r,
    raw_s, raw_r, v_s, v_r,
):
    me = lax.axis_index("rows")
    group = lax.axis_index("pairs")
    n = n_rows * n_pairs
    bw = x.shape[2]
    rows = x.shape[3]
    chunks = rows // step
    each = send.shape[1]
    count = n // 2
    side = me // (n_rows // 2)
    partner = lax.rem(me + n_rows // 2, n_rows)
    partner_k = partner * n_pairs + group
    first, n_own = owners(n_rows)
    owner = (me >= first) & (me < first + n_own)
    sizes = sizes_of(bw, n_own)

    def fetches(half, c):
        cols = pl.ds(half * 2 * bw, 2 * bw)
        part = pl.ds(c * step, step)
        pairs = ((obs_ref, obs_in), (est_ref, est_in), (mask_ref, mask_in))
        return [
            pltpu.make_async_copy(src.at[part, cols], dst.at[part, cols], in_sem.at[half, c, i])
            for i, (src, dst) in enumerate(pairs)
        ]

    def fetch_start(half):
        for c in range(chunks):
            for fetch in fetches(half, c):
                fetch.start()

    fetch_start(1)

    barrier = pltpu.get_barrier_semaphore()
    my_k = me * n_pairs + group

    def greet(i, carry):
        k = lax.rem(my_k + i, n)
        pl.semaphore_signal(
            barrier, inc=1, device_id=(k // n_pairs, lax.rem(k, n_pairs)), device_id_type=MESH
        )
        return carry

    lax.fori_loop(1, n, greet, 0)

    fetch_start(0)

    def fill_gram(half):
        total = jnp.zeros((2 * bw, 2 * bw), F32)
        for c in range(chunks):
            part = slice(c * step, (c + 1) * step)
            for fetch in fetches(half, c):
                fetch.wait()
            for slot in (2 * half, 2 * half + 1):
                cols = slice(slot * bw, (slot + 1) * bw)
                filled = jnp.where(mask_in[part, cols] == 1, obs_in[part, cols], est_in[part, cols])
                x[0, slot, :, part] = filled.T
            both = split(jnp.concatenate([x[0, 2 * half, :, part], x[0, 2 * half + 1, :, part]], axis=0))
            total += dot_parts(both, both, NT)
        return total

    def cross_gram(s, m):
        total = jnp.zeros((2 * bw, 2 * bw), F32)
        for c in range(chunks):
            part = slice(c * step, (c + 1) * step)
            s_parts = jnp.concatenate(split(s[:, part]), axis=0)
            m_parts = jnp.concatenate(split(m[:, part]), axis=0)
            total += lax.dot_general(s_parts, m_parts, NT, preferred_element_type=F32)
        return total[:bw, :bw] + (total[:bw, bw:] + total[bw:, :bw])

    def place(b):
        return sum(sizes[:b]), sum(sizes[:b]) // n_own, sizes[b] // n_own

    def own(b, q):
        base, _, piece = place(b)
        return pl.ds(pl.multiple_of(base + q * piece, 8), piece)

    def fill_pay(b, blocks):
        at = place(b)[0]
        for block in blocks:
            pay[at : at + block.shape[0], :] = block
            at += block.shape[0]

    def reduce_start(b, blocks=()):
        _, lbase, piece = place(b)
        fill_pay(b, blocks)
        if b == 0:
            pl.semaphore_wait(barrier, n - 1)

        def scatter(i, carry):
            q = lax.rem(me + i, n_own)
            peer = first + q

            @pl.when(peer != me)
            def _():
                pltpu.make_async_remote_copy(
                    pay.at[own(b, q)], land.at[lax.rem(me + n_rows - peer, n_rows), pl.ds(lbase, piece)],
                    rs_s.at[b], rs_r.at[b], device_id=(peer, group), device_id_type=MESH,
                ).start()

            return carry

        lax.fori_loop(0, n_own, scatter, 0)

    def wait_pieces(b, some, sem):
        _, lbase, piece = place(b)
        ref = land.at[pl.ds(0, some), pl.ds(lbase, piece)]
        pltpu.make_async_copy(ref, ref, sem).wait()

    def reduce_mid(b):
        _, lbase, piece = place(b)

        @pl.when(owner)
        def _():
            wait_pieces(b, n_rows - 1, rs_r.at[b])
            mine = own(b, me - first)
            total = pay[mine, :]
            for off in range(1, n_rows):
                total += land[off, lbase : lbase + piece, :]
            res[mine, :] = total

            def gather(off, carry):
                peer = lax.rem(me + off, n_rows)
                pltpu.make_async_remote_copy(
                    res.at[mine], res.at[mine],
                    ag_s.at[b], ag_r.at[b], device_id=(peer, group), device_id_type=MESH,
                ).start()
                return carry

            lax.fori_loop(1, n_rows, gather, 0)

    def pieces_to_owners(b, sem):
        @pl.when(owner)
        def _():
            wait_pieces(b, n_own - 1, sem)

        @pl.when(jnp.logical_not(owner))
        def _():
            wait_pieces(b, n_own, sem)

    def reduce_end(b):
        base, _, _ = place(b)
        pieces_to_owners(b, ag_r.at[b])
        return res[base : base + sizes[b], :]

    def settle(b):
        pieces_to_owners(b, rs_s.at[b])

        @pl.when(owner)
        def _():
            wait_pieces(b, n_rows - 1, ag_s.at[b])

    def put(v_parts, s, m, write, start=0, stop=None):
        stop = s.shape[1] if stop is None else stop
        for at in range(start, stop, step):
            part = slice(at, min(at + step, stop))
            both = split(jnp.concatenate([s[:, part], m[:, part]], axis=0))
            write(part, dot_parts(v_parts, both, NN))

    def into(ref):
        def write(part, value):
            ref[:, part] = value
        return write

    right = lax.rem(group + 1, n_pairs)

    def pass_copy(src, dst, send_sem, recv_sem):
        return pltpu.make_async_remote_copy(
            src, dst, send_sem, recv_sem, device_id=(me, right), device_id_type=MESH
        )

    skip = (ahead, 0, 0)

    def put_and_pass(i, v_half, s, m):
        def write(part, value):
            keep[i, :, part] = value
            pass_copy(
                keep.at[i, :, part], x.at[i + 1, 1, :, part], pm_s.at[i], pm_r.at[i]
            ).start()

        put(split(v_half), s, m, write, skip[i])

    def pass_gram(i, gmm):
        gmm_out[i] = gmm
        small = pass_copy(gmm_out.at[i], gmm_in.at[i], pg_s.at[i], pg_r.at[i])
        small.start()
        main = pass_copy(
            keep.at[i, :, skip[i] :], x.at[i + 1, 1, :, skip[i] :], pm_s.at[i], pm_r.at[i]
        )
        return main, small

    raw_copy = pass_copy(x.at[0, 2:4, :, :ahead], raw, raw_s, raw_r)
    odd = lax.rem(me, 2)
    sibling = me + 1 - 2 * odd
    mine_v = pl.ds(pl.multiple_of(odd * (bw // 2), 8), bw // 2)
    other_v = pl.ds(pl.multiple_of((1 - odd) * (bw // 2), 8), bw // 2)
    v_pass = pass_copy(v_out.at[mine_v], v_in.at[mine_v], v_s.at[0], v_r.at[0])
    v_share = pltpu.make_async_remote_copy(
        v_in.at[mine_v], v_in.at[mine_v], v_s.at[1], v_r.at[1],
        device_id=(sibling, group), device_id_type=MESH,
    )
    v_shared = pltpu.make_async_remote_copy(
        v_in.at[other_v], v_in.at[other_v], v_s.at[1], v_r.at[1],
        device_id=(sibling, group), device_id_type=MESH,
    )

    def new_grams(v, gram):
        vg = dot3(v, gram)
        return dot3(vg[:bw], v[:bw], NT), dot3(vg[bw:], v[bw:], NT)

    n_early = early // 128

    def far_copy(half, j, at, size):
        return pltpu.make_async_remote_copy(
            x.at[3, 2 * half + j, :, pl.ds(at, size)], far.at[j, :, pl.ds(at, size)],
            far_s.at[j], far_r.at[j], device_id=(partner, group), device_id_type=MESH,
        )

    shipped = [0, 0]

    def ship(half, some):
        for i in range(shipped[half], min(shipped[half] + some, 2 * n_early)):
            @pl.when(side != half)
            def _():
                far_copy(half, i // n_early, i % n_early * 128, 128).start()
        shipped[half] += some

    def scale_last(half, v, gram):
        vg = dot3(v, gram)
        squares = jnp.sum(vg * v, axis=1, keepdims=True)
        norm = jnp.sqrt(squares + 1e-06)
        eye = (
            lax.broadcasted_iota(jnp.int32, gram.shape, 0)
            == lax.broadcasted_iota(jnp.int32, gram.shape, 1)
        )
        level = thr_ref[:, 2 * half * bw : 2 * (half + 1) * bw]
        level = jnp.sum(jnp.where(eye, level, 0.0), axis=1, keepdims=True)
        last_hi[half], last_lo[half] = split((jnp.maximum(norm - level, 0.0) / norm) * v)

    per_block = bw // each

    def finish(half, target, base, s, m, start, stop):
        for j in range(2):
            def write(part, value):
                for i in range(per_block):
                    target[base + j * per_block + i, :, part] = value[i * each : (i + 1) * each]

            cut = slice(j * bw, (j + 1) * bw)
            put((last_hi[half, cut], last_lo[half, cut]), s, m, write, start, stop)

    def to(k):
        return dict(device_id=(k // n_pairs, lax.rem(k, n_pairs)), device_id_type=MESH)

    def deliver(half, same):
        def go(i, carry):
            k = half * count + lax.rem(my_k + i, count)
            if not same:
                pltpu.make_async_remote_copy(
                    send.at[k, :, early:], out_ref.at[my_k, :, early:], out_s.at[1], out_r.at[1], **to(k)
                ).start()
                return carry

            @pl.when(k != my_k)
            def _():
                pltpu.make_async_remote_copy(
                    send.at[k], out_ref.at[my_k], out_s.at[0], out_r.at[0], **to(k)
                ).start()

            @pl.when(k == my_k)
            def _():
                pltpu.make_async_copy(send.at[k], out_ref.at[my_k], own_sem.at[0]).start()

            return carry

        lax.fori_loop(0, count, go, 0)

    def deliver_onward():
        def go(i, carry):
            at = lax.rem(my_k + i, count)
            k = side * count + at
            spot = out_ref.at[partner_k, :, :early]

            @pl.when(k != my_k)
            def _():
                pltpu.make_async_remote_copy(
                    onward.at[at], spot, out_s.at[2], out_r.at[2], **to(k)
                ).start()

            @pl.when(k == my_k)
            def _():
                pltpu.make_async_copy(onward.at[at], spot, own_sem.at[1]).start()

            return carry

        lax.fori_loop(0, count, go, 0)

    def compute_last(half):
        s, m = x.at[3, 2 * half], x.at[3, 2 * half + 1]
        finish(half, send, half * count, s, m, early, rows)

        @pl.when(side == half)
        def _():
            finish(half, send, half * count, s, m, 0, early)

    def deliver_last(half):
        @pl.when(side != half)
        def _():
            deliver(half, False)

        @pl.when(side == half)
        def _():
            deliver(half, True)

    reduce_start(0, pack(fill_gram(1), n_own))
    raw_copy.start()
    fill_pay(1, pack(fill_gram(0), n_own))
    reduce_start(1)
    reduce_mid(0)
    reduce_mid(1)
    gb = unpack(reduce_end(0))
    vb = whitening_t(gb)
    v_out[...] = vb[bw:]
    v_pass.start()
    put_and_pass(0, vb[bw:], x.at[0, 2], x.at[0, 3])
    bs, bm = new_grams(vb, gb)
    sent = [pass_gram(0, bm)]
    put(split(vb[:bw]), x.at[0, 2], x.at[0, 3], into(x.at[1, 2]))
    ga = unpack(reduce_end(1))
    va = whitening_t(ga)
    put(split(va[bw:]), x.at[0, 0], x.at[0, 1], into(x.at[1, 3]))

    reduce_start(2, [cross_gram(x.at[1, 2], x.at[1, 3])])
    put(split(va[:bw]), x.at[0, 0], x.at[0, 1], into(x.at[1, 0]))
    v_pass.wait_recv()
    v_share.start()
    as_, am = new_grams(va, ga)
    reduce_mid(2)
    gb = join(bs, reduce_end(2), am)
    vb = whitening_t(gb)
    put_and_pass(1, vb[bw:], x.at[1, 2], x.at[1, 3])
    raw_copy.wait_recv()
    v_shared.wait_recv()
    put(split(v_in[...]), raw.at[0], raw.at[1], into(x.at[1, 1]))
    for c in sent[0]:
        c.wait_recv()
    reduce_start(3, [cross_gram(x.at[1, 0], x.at[1, 1])])
    bs, bm = new_grams(vb, gb)
    sent.append(pass_gram(1, bm))
    put(split(vb[:bw]), x.at[1, 2], x.at[1, 3], into(x.at[2, 2]))
    reduce_mid(3)
    ga = join(as_, reduce_end(3), gmm_in[0])
    va = whitening_t(ga)
    put(split(va[bw:]), x.at[1, 0], x.at[1, 1], into(x.at[2, 3]))

    reduce_start(4, [cross_gram(x.at[2, 2], x.at[2, 3])])
    put(split(va[:bw]), x.at[1, 0], x.at[1, 1], into(x.at[2, 0]))
    as_, am = new_grams(va, ga)
    reduce_mid(4)
    for c in sent[1]:
        c.wait_recv()
    reduce_start(5, [cross_gram(x.at[2, 0], x.at[2, 1])])
    gb = join(bs, reduce_end(4), am)
    vb = whitening_t(gb)
    put_and_pass(2, vb[bw:], x.at[2, 2], x.at[2, 3])
    bs, bm = new_grams(vb, gb)
    sent.append(pass_gram(2, bm))
    put(split(vb[:bw]), x.at[2, 2], x.at[2, 3], into(x.at[3, 2]))
    ship(1, SHIP[0])
    reduce_mid(5)
    ship(1, SHIP[1])
    ga = join(as_, reduce_end(5), gmm_in[1])
    va = whitening_t(ga)
    put(split(va[bw:]), x.at[2, 0], x.at[2, 1], into(x.at[3, 3]))

    reduce_start(6, [cross_gram(x.at[3, 2], x.at[3, 3])])
    ship(1, SHIP[2])
    put(split(va[:bw]), x.at[2, 0], x.at[2, 1], into(x.at[3, 0]))
    ship(0, SHIP[3])
    as_, am = new_grams(va, ga)
    reduce_mid(6)
    ship(1, SHIP[4])
    ship(0, min(SHIP[5], n_early - SHIP[3]))
    for c in sent[2]:
        c.wait_recv()
    reduce_start(7, [cross_gram(x.at[3, 0], x.at[3, 1])])
    ship(1, SHIP[6])
    ship(0, SHIP[7])
    gb = join(bs, reduce_end(6), am)
    scale_last(1, whitening_t(gb), gb)
    compute_last(1)
    reduce_mid(7)
    ship(1, 2 * n_early)
    ship(0, 2 * n_early)
    ga = join(as_, reduce_end(7), gmm_in[2])
    deliver_last(1)
    scale_last(0, whitening_t(ga), ga)
    compute_last(0)
    deliver_last(0)
    for half in (1, 0):
        @pl.when(side == half)
        def _():
            for j in range(2):
                far_copy(half, j, 0, early).wait_recv()
            finish(half, onward, 0, far.at[0], far.at[1], 0, early)
            deliver_onward()

    for b in range(len(sizes)):
        settle(b)
    for pair in sent:
        for c in pair:
            c.wait_send()
    raw_copy.wait_send()
    v_pass.wait_send()
    v_share.wait_send()
    for j in range(2):
        far_copy(0, j, 0, early).wait_send()
    pltpu.make_async_copy(send.at[0], out_ref.at[my_k], own_sem.at[0]).wait()
    pltpu.make_async_copy(onward.at[0], out_ref.at[my_k, :, :early], own_sem.at[1]).wait()
    for ref, sems in ((send, out_s), (out_ref, out_r)):
        for i, some in enumerate((
            ref.at[pl.ds(0, count - 1)],
            ref.at[pl.ds(0, count), :, early:],
            ref.at[pl.ds(0, count - 1), :, :early],
        )):
            pltpu.make_async_copy(some, some, sems.at[i]).wait()


def interleave(in_ref, out_ref, taken, mixed, in_sem, out_sem):
    n_rows, n_pairs, each, rows = in_ref.shape
    ins = [pltpu.make_async_copy(in_ref.at[r], taken.at[r], in_sem.at[r]) for r in range(n_rows)]
    for copy in ins:
        copy.start()
    outs = []
    for r in range(n_rows):
        cols = slice(r * rows, (r + 1) * rows)
        ins[r].wait()
        for i in range(each):
            mixed[i * n_pairs : (i + 1) * n_pairs, cols] = taken[r, :, i, :]
        outs.append(pltpu.make_async_copy(mixed.at[:, cols], out_ref.at[:, cols], out_sem.at[r]))
        outs[-1].start()
    for copy in outs:
        copy.wait()


SHIP = (1, 1, 2, 1, 1, 3, 2, 1)


def on_device(observed, estimate, mask, threshold):
    n_rows = lax.axis_size("rows")
    n_pairs = lax.axis_size("pairs")
    rows, width = observed.shape
    bw = width // 4
    n = n_rows * n_pairs
    each = width // n
    step = 512 if rows % 512 == 0 else rows
    early = rows * 4 // 12 // 128 * 128 or rows
    ahead = rows * 5 // 12 // 128 * 128 or rows
    n_own = owners(n_rows)[1]
    sizes = sizes_of(bw, n_own)
    total = sum(sizes)
    vmem = pl.BlockSpec(memory_space=pltpu.VMEM)
    dma = pltpu.SemaphoreType.DMA
    nb = len(sizes)
    landed = pl.pallas_call(
        functools.partial(kernel, n_rows, n_pairs, step, early, ahead),
        out_shape=jax.ShapeDtypeStruct((n, each, rows), F32),
        in_specs=[pl.BlockSpec(memory_space=pl.ANY)] * 3 + [vmem],
        out_specs=pl.BlockSpec(memory_space=pl.ANY),
        scratch_shapes=[
            pltpu.VMEM((rows, width), F32),
            pltpu.VMEM((rows, width), F32),
            pltpu.VMEM((rows, width), jnp.int32),
            pltpu.VMEM((4, 4, bw, rows), F32),
            pltpu.VMEM((3, bw, rows), F32),
            pltpu.VMEM((total, bw), F32),
            pltpu.VMEM((n_rows, total // n_own, bw), F32),
            pltpu.VMEM((total, bw), F32),
            pltpu.VMEM((3, bw, bw), F32),
            pltpu.VMEM((3, bw, bw), F32),
            pltpu.VMEM((2, 2 * bw, 2 * bw), BF16),
            pltpu.VMEM((2, 2 * bw, 2 * bw), BF16),
            pltpu.VMEM((n, each, rows), F32),
            pltpu.VMEM((2, bw, early), F32),
            pltpu.VMEM((n // 2, each, early), F32),
            pltpu.VMEM((2, bw, ahead), F32),
            pltpu.VMEM((bw, 2 * bw), F32),
            pltpu.VMEM((bw, 2 * bw), F32),
            dma((nb,)), dma((nb,)), dma((nb,)), dma((nb,)),
            dma((3,)), dma((3,)), dma((3,)), dma((3,)),
            dma((3,)), dma((3,)), dma((2,)), dma((2, rows // step, 3)), dma((2,)), dma((2,)),
            dma, dma, dma((2,)), dma((2,)),
        ],
        compiler_params=pltpu.CompilerParams(
            collective_id=0, has_side_effects=True, vmem_limit_bytes=60 * 1024 * 1024
        ),
    )(observed, estimate, mask, threshold.reshape(1, width))
    landed = landed.reshape(n_rows, n_pairs, each, rows)
    return pl.pallas_call(
        interleave,
        out_shape=jax.ShapeDtypeStruct((each * n_pairs, n_rows * rows), F32),
        in_specs=[pl.BlockSpec(memory_space=pl.ANY)],
        out_specs=pl.BlockSpec(memory_space=pl.ANY),
        scratch_shapes=[
            pltpu.VMEM((n_rows, n_pairs, each, rows), F32),
            pltpu.VMEM((each * n_pairs, n_rows * rows), F32),
            dma((n_rows,)), dma((n_rows,)),
        ],
    )(landed)


def solution(mesh):
    placed = (P("rows", "pairs"), P("rows", "pairs"), P("rows", "pairs"), P("pairs"))
    return jax.shard_map(
        on_device, mesh=mesh, in_specs=placed, out_specs=P(("rows", "pairs"), None), check_vma=False
    )
```

```python
import functools

import jax
import jax.numpy as jnp
from jax import lax
from jax.experimental import pallas as pl
from jax.experimental.pallas import tpu as pltpu
from jax.sharding import PartitionSpec as P

MESH = pl.DeviceIdType.MESH
F32 = jnp.float32
BF16 = jnp.bfloat16
NN = (((1,), (0,)), ((), ()))
NT = (((1,), (1,)), ((), ()))


def split(a):
    high = a.astype(BF16)
    return high, (a - high.astype(F32)).astype(BF16)


def dot_parts(a, b, dims):
    def one(x, y):
        return lax.dot_general(x, y, dims, preferred_element_type=F32)

    return one(a[0], b[0]) + (one(a[0], b[1]) + one(a[1], b[0]))


def dot3(a, b, dims=NN):
    return dot_parts(split(a), split(b), dims)


def whitening_t(gram):
    width = gram.shape[0]
    eye = (
        lax.broadcasted_iota(jnp.int32, (width, width), 0)
        == lax.broadcasted_iota(jnp.int32, (width, width), 1)
    ).astype(F32)
    on_diag = gram * eye
    d_col = jnp.sum(on_diag, axis=1, keepdims=True) + 1e-06
    d_row = jnp.sum(on_diag, axis=0, keepdims=True) + 1e-06
    i_col = 1.0 / jnp.sqrt(d_col)
    i_row = 1.0 / jnp.sqrt(d_row)
    normed = gram * i_col * i_row
    sq = jnp.sum(jnp.sum(normed * normed, axis=0, keepdims=True), axis=1, keepdims=True)
    fro = jnp.sqrt(sq)
    y = normed / fro
    square_y = dot3(y, y)
    t = 1.5 * eye - 0.5 * y
    square_t = 2.25 * eye - 1.5 * y + 0.25 * square_y
    zy, zyt = dot3(y, square_t), dot3(1.5 * y - 0.5 * square_y, square_t)
    t_next = 1.5 * eye - 0.5 * zy
    z, tail, square_t = dot3(t, t_next), dot3(zyt, t_next), dot3(t_next, t_next)
    z = 1.5 * z - 0.5 * dot3(tail, square_t)
    return jnp.sqrt(d_col) * z * i_row / jnp.sqrt(fro)


def join(ss, sm, mm):
    top = jnp.concatenate([ss, sm], axis=1)
    low = jnp.concatenate([sm.T, mm], axis=1)
    return jnp.concatenate([top, low], axis=0)


def square(width):
    shape = (width, width)
    return lax.broadcasted_iota(jnp.int32, shape, 0), lax.broadcasted_iota(jnp.int32, shape, 1)


def pack(gram, n_own):
    bw = gram.shape[0] // 2
    ss, sm, mm = gram[:bw, :bw], gram[:bw, bw:], gram[bw:, bw:]
    r, c = square(bw)
    diag = jnp.sum(jnp.where(r == c, mm, 0.0), axis=0, keepdims=True)
    return [jnp.where(r <= c, ss, mm), sm, jnp.broadcast_to(diag, (8 * n_own, bw))]


def unpack(packed):
    bw = packed.shape[1]
    both, sm, diag = packed[:bw], packed[bw : 2 * bw], packed[2 * bw : 2 * bw + 1]
    r, c = square(bw)
    flip = both.T
    mm = jnp.where(r == c, diag, jnp.where(r > c, both, flip))
    return join(jnp.where(r <= c, both, flip), sm, mm)


def owners(n_rows):
    if n_rows % 4:
        return [(0, n_rows)] * 8
    return [(n_rows // 4, n_rows // 2)] * 8


def sizes_of(bw, n_own):
    return [2 * bw + 8 * n_own] * 2 + [bw] * 6


def pieces_of(sizes, owned):
    return [size // n_own for size, (_, n_own) in zip(sizes, owned)]


def kernel(
    n_rows, n_pairs, step, early, ahead,
    obs_ref, est_ref, mask_ref, thr_ref, out_ref,
    obs_in, est_in, mask_in, x, keep, pay, land, res, gmm_out, gmm_in, last_hi, last_lo, send, far, onward, raw, v_out, v_in,
    rs_s, rs_r, ag_s, ag_r, pm_s, pm_r, pg_s, pg_r, out_s, out_r, own_sem, in_sem, far_s, far_r,
    raw_s, raw_r, v_s, v_r,
):
    me = lax.axis_index("rows")
    group = lax.axis_index("pairs")
    n = n_rows * n_pairs
    bw = x.shape[2]
    rows = x.shape[3]
    chunks = rows // step
    each = send.shape[1]
    count = n // 2
    side = me // (n_rows // 2)
    partner = lax.rem(me + n_rows // 2, n_rows)
    partner_k = partner * n_pairs + group
    owned = owners(n_rows)
    sizes = sizes_of(bw, owned[0][1])

    def fetches(half, c):
        cols = pl.ds(half * 2 * bw, 2 * bw)
        part = pl.ds(c * step, step)
        pairs = ((obs_ref, obs_in), (est_ref, est_in), (mask_ref, mask_in))
        return [
            pltpu.make_async_copy(src.at[part, cols], dst.at[part, cols], in_sem.at[half, c, i])
            for i, (src, dst) in enumerate(pairs)
        ]

    def fetch_start(half):
        for c in range(chunks):
            for fetch in fetches(half, c):
                fetch.start()

    fetch_start(1)

    barrier = pltpu.get_barrier_semaphore()
    my_k = me * n_pairs + group

    def greet(i, carry):
        k = lax.rem(my_k + i, n)
        pl.semaphore_signal(
            barrier, inc=1, device_id=(k // n_pairs, lax.rem(k, n_pairs)), device_id_type=MESH
        )
        return carry

    lax.fori_loop(1, n, greet, 0)

    fetch_start(0)

    def fill_gram(half):
        total = jnp.zeros((2 * bw, 2 * bw), F32)
        for c in range(chunks):
            part = slice(c * step, (c + 1) * step)
            for fetch in fetches(half, c):
                fetch.wait()
            for slot in (2 * half, 2 * half + 1):
                cols = slice(slot * bw, (slot + 1) * bw)
                filled = jnp.where(mask_in[part, cols] == 1, obs_in[part, cols], est_in[part, cols])
                x[0, slot, :, part] = filled.T
            both = split(jnp.concatenate([x[0, 2 * half, :, part], x[0, 2 * half + 1, :, part]], axis=0))
            total += dot_parts(both, both, NT)
        return total

    def cross_gram(s, m):
        total = jnp.zeros((2 * bw, 2 * bw), F32)
        for c in range(chunks):
            part = slice(c * step, (c + 1) * step)
            s_parts = jnp.concatenate(split(s[:, part]), axis=0)
            m_parts = jnp.concatenate(split(m[:, part]), axis=0)
            total += lax.dot_general(s_parts, m_parts, NT, preferred_element_type=F32)
        return total[:bw, :bw] + (total[:bw, bw:] + total[bw:, :bw])

    def place(b):
        pieces = pieces_of(sizes, owned)
        return sum(sizes[:b]), sum(pieces[:b]), pieces[b]

    def owner(b):
        first, n_own = owned[b]
        return (me >= first) & (me < first + n_own)

    def own(b, q):
        base, _, piece = place(b)
        return pl.ds(pl.multiple_of(base + q * piece, 8), piece)

    def fill_pay(b, blocks):
        at = place(b)[0]
        for block in blocks:
            pay[at : at + block.shape[0], :] = block
            at += block.shape[0]

    def reduce_start(b, blocks=()):
        _, lbase, piece = place(b)
        first, n_own = owned[b]
        fill_pay(b, blocks)
        if b == 0:
            pl.semaphore_wait(barrier, n - 1)

        def scatter(i, carry):
            q = lax.rem(me + i, n_own)
            peer = first + q

            @pl.when(peer != me)
            def _():
                pltpu.make_async_remote_copy(
                    pay.at[own(b, q)], land.at[lax.rem(me + n_rows - peer, n_rows), pl.ds(lbase, piece)],
                    rs_s.at[b], rs_r.at[b], device_id=(peer, group), device_id_type=MESH,
                ).start()

            return carry

        lax.fori_loop(0, n_own, scatter, 0)

    def wait_pieces(b, some, sem):
        _, lbase, piece = place(b)
        ref = land.at[pl.ds(0, some), pl.ds(lbase, piece)]
        pltpu.make_async_copy(ref, ref, sem).wait()

    def reduce_mid(b):
        _, lbase, piece = place(b)

        @pl.when(owner(b))
        def _():
            wait_pieces(b, n_rows - 1, rs_r.at[b])
            mine = own(b, me - owned[b][0])
            total = pay[mine, :]
            for off in range(1, n_rows):
                total += land[off, lbase : lbase + piece, :]
            res[mine, :] = total

            def gather(off, carry):
                peer = lax.rem(me + off, n_rows)
                pltpu.make_async_remote_copy(
                    res.at[mine], res.at[mine],
                    ag_s.at[b], ag_r.at[b], device_id=(peer, group), device_id_type=MESH,
                ).start()
                return carry

            lax.fori_loop(1, n_rows, gather, 0)

    def pieces_to_owners(b, sem):
        @pl.when(owner(b))
        def _():
            if owned[b][1] > 1:
                wait_pieces(b, owned[b][1] - 1, sem)

        @pl.when(jnp.logical_not(owner(b)))
        def _():
            wait_pieces(b, owned[b][1], sem)

    def reduce_end(b):
        base, _, _ = place(b)
        pieces_to_owners(b, ag_r.at[b])
        return res[base : base + sizes[b], :]

    def settle(b):
        pieces_to_owners(b, rs_s.at[b])

        @pl.when(owner(b))
        def _():
            wait_pieces(b, n_rows - 1, ag_s.at[b])

    def put(v_parts, s, m, write, start=0, stop=None):
        stop = s.shape[1] if stop is None else stop
        for at in range(start, stop, step):
            part = slice(at, min(at + step, stop))
            both = split(jnp.concatenate([s[:, part], m[:, part]], axis=0))
            write(part, dot_parts(v_parts, both, NN))

    def into(ref):
        def write(part, value):
            ref[:, part] = value
        return write

    right = lax.rem(group + 1, n_pairs)

    def pass_copy(src, dst, send_sem, recv_sem):
        return pltpu.make_async_remote_copy(
            src, dst, send_sem, recv_sem, device_id=(me, right), device_id_type=MESH
        )

    skip = (ahead, 0, 0)

    def put_and_pass(i, v_half, s, m):
        def write(part, value):
            keep[i, :, part] = value
            pass_copy(
                keep.at[i, :, part], x.at[i + 1, 1, :, part], pm_s.at[i], pm_r.at[i]
            ).start()

        put(split(v_half), s, m, write, skip[i])

    def pass_gram(i, gmm):
        gmm_out[i] = gmm
        small = pass_copy(gmm_out.at[i], gmm_in.at[i], pg_s.at[i], pg_r.at[i])
        small.start()
        main = pass_copy(
            keep.at[i, :, skip[i] :], x.at[i + 1, 1, :, skip[i] :], pm_s.at[i], pm_r.at[i]
        )
        return main, small

    raw_copy = pass_copy(x.at[0, 2:4, :, :ahead], raw, raw_s, raw_r)
    odd = lax.rem(me, 2)
    sibling = me + 1 - 2 * odd
    mine_v = pl.ds(pl.multiple_of(odd * (bw // 2), 8), bw // 2)
    other_v = pl.ds(pl.multiple_of((1 - odd) * (bw // 2), 8), bw // 2)
    v_pass = pass_copy(v_out.at[mine_v], v_in.at[mine_v], v_s.at[0], v_r.at[0])
    v_share = pltpu.make_async_remote_copy(
        v_in.at[mine_v], v_in.at[mine_v], v_s.at[1], v_r.at[1],
        device_id=(sibling, group), device_id_type=MESH,
    )
    v_shared = pltpu.make_async_remote_copy(
        v_in.at[other_v], v_in.at[other_v], v_s.at[1], v_r.at[1],
        device_id=(sibling, group), device_id_type=MESH,
    )

    def new_grams(v, gram):
        vg = dot3(v, gram)
        return dot3(vg[:bw], v[:bw], NT), dot3(vg[bw:], v[bw:], NT)

    def far_copy(half, j, at, size):
        return pltpu.make_async_remote_copy(
            x.at[3, 2 * half + j, :, pl.ds(at, size)], far.at[j, :, pl.ds(at, size)],
            far_s.at[j], far_r.at[j], device_id=(partner, group), device_id_type=MESH,
        )

    shipped = [0, 0]

    def ship(half, some):
        n_early = early[half] // 128
        upto = min(shipped[half] + some, 2 * n_early)

        @pl.when(side != half)
        def _():
            for i in range(shipped[half], upto):
                far_copy(half, i // n_early, i % n_early * 128, 128).start()

        shipped[half] = upto

    def scale_last(half, v, gram):
        vg = dot3(v, gram)
        squares = jnp.sum(vg * v, axis=1, keepdims=True)
        norm = jnp.sqrt(squares + 1e-06)
        eye = (
            lax.broadcasted_iota(jnp.int32, gram.shape, 0)
            == lax.broadcasted_iota(jnp.int32, gram.shape, 1)
        )
        level = thr_ref[:, 2 * half * bw : 2 * (half + 1) * bw]
        level = jnp.sum(jnp.where(eye, level, 0.0), axis=1, keepdims=True)
        last_hi[half], last_lo[half] = split((jnp.maximum(norm - level, 0.0) / norm) * v)

    per_block = bw // each

    def finish(half, target, base, s, m, start, stop):
        for j in range(2):
            def write(part, value):
                for i in range(per_block):
                    target[base + j * per_block + i, :, part] = value[i * each : (i + 1) * each]

            cut = slice(j * bw, (j + 1) * bw)
            put((last_hi[half, cut], last_lo[half, cut]), s, m, write, start, stop)

    def to(k):
        return dict(device_id=(k // n_pairs, lax.rem(k, n_pairs)), device_id_type=MESH)

    def deliver(half, same):
        def go(i, carry):
            k = half * count + lax.rem(my_k + i, count)
            if not same:
                pltpu.make_async_remote_copy(
                    send.at[k, :, early[half] :], out_ref.at[my_k, :, early[half] :],
                    out_s.at[1], out_r.at[1], **to(k)
                ).start()
                return carry

            @pl.when(k != my_k)
            def _():
                pltpu.make_async_remote_copy(
                    send.at[k], out_ref.at[my_k], out_s.at[0], out_r.at[0], **to(k)
                ).start()

            @pl.when(k == my_k)
            def _():
                pltpu.make_async_copy(send.at[k], out_ref.at[my_k], own_sem.at[0]).start()

            return carry

        lax.fori_loop(0, count, go, 0)

    def deliver_onward(half):
        def go(i, carry):
            at = lax.rem(my_k + i, count)
            k = half * count + at
            some = onward.at[at, :, : early[half]]
            spot = out_ref.at[partner_k, :, : early[half]]

            @pl.when(k != my_k)
            def _():
                pltpu.make_async_remote_copy(
                    some, spot, out_s.at[2], out_r.at[2], **to(k)
                ).start()

            @pl.when(k == my_k)
            def _():
                pltpu.make_async_copy(some, spot, own_sem.at[1]).start()

            return carry

        lax.fori_loop(0, count, go, 0)

    def compute_last(half):
        s, m = x.at[3, 2 * half], x.at[3, 2 * half + 1]
        finish(half, send, half * count, s, m, early[half], rows)

        @pl.when(side == half)
        def _():
            finish(half, send, half * count, s, m, 0, early[half])

    def deliver_other(half):
        @pl.when(side != half)
        def _():
            deliver(half, False)

    def deliver_own(half):
        @pl.when(side == half)
        def _():
            deliver(half, True)

    reduce_start(0, pack(fill_gram(1), owned[0][1]))
    raw_copy.start()
    fill_pay(1, pack(fill_gram(0), owned[1][1]))
    reduce_start(1)
    reduce_mid(0)
    reduce_mid(1)
    gb = unpack(reduce_end(0))
    vb = whitening_t(gb)
    v_out[...] = vb[bw:]
    v_pass.start()
    put_and_pass(0, vb[bw:], x.at[0, 2], x.at[0, 3])
    bs, bm = new_grams(vb, gb)
    sent = [pass_gram(0, bm)]
    put(split(vb[:bw]), x.at[0, 2], x.at[0, 3], into(x.at[1, 2]))
    ga = unpack(reduce_end(1))
    va = whitening_t(ga)
    put(split(va[bw:]), x.at[0, 0], x.at[0, 1], into(x.at[1, 3]))

    reduce_start(2, [cross_gram(x.at[1, 2], x.at[1, 3])])
    put(split(va[:bw]), x.at[0, 0], x.at[0, 1], into(x.at[1, 0]))
    v_pass.wait_recv()
    v_share.start()
    as_, am = new_grams(va, ga)
    reduce_mid(2)
    gb = join(bs, reduce_end(2), am)
    vb = whitening_t(gb)
    put_and_pass(1, vb[bw:], x.at[1, 2], x.at[1, 3])
    raw_copy.wait_recv()
    v_shared.wait_recv()
    put(split(v_in[...]), raw.at[0], raw.at[1], into(x.at[1, 1]))
    for c in sent[0]:
        c.wait_recv()
    reduce_start(3, [cross_gram(x.at[1, 0], x.at[1, 1])])
    bs, bm = new_grams(vb, gb)
    sent.append(pass_gram(1, bm))
    put(split(vb[:bw]), x.at[1, 2], x.at[1, 3], into(x.at[2, 2]))
    reduce_mid(3)
    ga = join(as_, reduce_end(3), gmm_in[0])
    va = whitening_t(ga)
    put(split(va[bw:]), x.at[1, 0], x.at[1, 1], into(x.at[2, 3]))

    reduce_start(4, [cross_gram(x.at[2, 2], x.at[2, 3])])
    put(split(va[:bw]), x.at[1, 0], x.at[1, 1], into(x.at[2, 0]))
    as_, am = new_grams(va, ga)
    reduce_mid(4)
    gb = join(bs, reduce_end(4), am)
    vb = whitening_t(gb)
    put_and_pass(2, vb[bw:], x.at[2, 2], x.at[2, 3])
    for c in sent[1]:
        c.wait_recv()
    reduce_start(5, [cross_gram(x.at[2, 0], x.at[2, 1])])
    bs, bm = new_grams(vb, gb)
    sent.append(pass_gram(2, bm))
    put(split(vb[:bw]), x.at[2, 2], x.at[2, 3], into(x.at[3, 2]))
    ship(1, SHIP[0])
    reduce_mid(5)
    ship(1, SHIP[1])
    ga = join(as_, reduce_end(5), gmm_in[1])
    va = whitening_t(ga)
    put(split(va[bw:]), x.at[2, 0], x.at[2, 1], into(x.at[3, 3]))

    reduce_start(6, [cross_gram(x.at[3, 2], x.at[3, 3])])
    ship(1, SHIP[2])
    put(split(va[:bw]), x.at[2, 0], x.at[2, 1], into(x.at[3, 0]))
    ship(0, SHIP[3])
    as_, am = new_grams(va, ga)
    reduce_mid(6)
    ship(1, SHIP[4])
    ship(0, min(SHIP[5], early[0] // 128 - SHIP[3]))
    for c in sent[2]:
        c.wait_recv()
    reduce_start(7, [cross_gram(x.at[3, 0], x.at[3, 1])])
    ship(1, SHIP[6])
    ship(0, SHIP[7])
    gb = join(bs, reduce_end(6), am)
    scale_last(1, whitening_t(gb), gb)
    compute_last(1)
    reduce_mid(7)
    ship(1, 2 * early[1] // 128)
    ship(0, 2 * early[0] // 128)
    ga = join(as_, reduce_end(7), gmm_in[2])
    deliver_other(1)
    deliver_own(1)
    scale_last(0, whitening_t(ga), ga)
    compute_last(0)
    deliver_other(0)
    deliver_own(0)
    for half in (1, 0):
        @pl.when(side == half)
        def _():
            for j in range(2):
                far_copy(half, j, 0, early[half]).wait_recv()
            finish(half, onward, 0, far.at[0], far.at[1], 0, early[half])
            deliver_onward(half)

    for b in range(len(sizes)):
        settle(b)
    for pair in sent:
        for c in pair:
            c.wait_send()
    raw_copy.wait_send()
    v_pass.wait_send()
    v_share.wait_send()
    pltpu.make_async_copy(send.at[0], out_ref.at[my_k], own_sem.at[0]).wait()

    def done(ref, sem):
        pltpu.make_async_copy(ref, ref, sem).wait()

    for half in (0, 1):
        @pl.when(side == half)
        def _():
            for j in range(2):
                far_copy(1 - half, j, 0, early[1 - half]).wait_send()
            done(onward.at[0, :, : early[half]], own_sem.at[1])
            done(send.at[pl.ds(0, count - 1)], out_s.at[0])
            done(send.at[pl.ds(0, count), :, early[1 - half] :], out_s.at[1])
            done(onward.at[pl.ds(0, count - 1), :, : early[half]], out_s.at[2])
            done(out_ref.at[pl.ds(0, count - 1)], out_r.at[0])
            done(out_ref.at[pl.ds(0, count), :, early[half] :], out_r.at[1])
            done(out_ref.at[pl.ds(0, count - 1), :, : early[half]], out_r.at[2])


def interleave(in_ref, out_ref, taken, mixed, in_sem, out_sem):
    n_rows, n_pairs, each, rows = in_ref.shape
    ins = [pltpu.make_async_copy(in_ref.at[r], taken.at[r], in_sem.at[r]) for r in range(n_rows)]
    for copy in ins:
        copy.start()
    outs = []
    for r in range(n_rows):
        cols = slice(r * rows, (r + 1) * rows)
        ins[r].wait()
        for i in range(each):
            mixed[i * n_pairs : (i + 1) * n_pairs, cols] = taken[r, :, i, :]
        outs.append(pltpu.make_async_copy(mixed.at[:, cols], out_ref.at[:, cols], out_sem.at[r]))
        outs[-1].start()
    for copy in outs:
        copy.wait()


EARLY = (4, 4)
SHIP = (1, 1, 2, 1, 1, 2, 1, 1)


def on_device(observed, estimate, mask, threshold):
    n_rows = lax.axis_size("rows")
    n_pairs = lax.axis_size("pairs")
    rows, width = observed.shape
    bw = width // 4
    n = n_rows * n_pairs
    each = width // n
    step = 512 if rows % 512 == 0 else rows
    early = [rows * part // 12 // 128 * 128 or rows for part in EARLY]
    ahead = rows * 5 // 12 // 128 * 128 or rows
    owned = owners(n_rows)
    sizes = sizes_of(bw, owned[0][1])
    total = sum(sizes)
    vmem = pl.BlockSpec(memory_space=pltpu.VMEM)
    dma = pltpu.SemaphoreType.DMA
    nb = len(sizes)
    landed = pl.pallas_call(
        functools.partial(kernel, n_rows, n_pairs, step, early, ahead),
        out_shape=jax.ShapeDtypeStruct((n, each, rows), F32),
        in_specs=[pl.BlockSpec(memory_space=pl.ANY)] * 3 + [vmem],
        out_specs=pl.BlockSpec(memory_space=pl.ANY),
        scratch_shapes=[
            pltpu.VMEM((rows, width), F32),
            pltpu.VMEM((rows, width), F32),
            pltpu.VMEM((rows, width), jnp.int32),
            pltpu.VMEM((4, 4, bw, rows), F32),
            pltpu.VMEM((3, bw, rows), F32),
            pltpu.VMEM((total, bw), F32),
            pltpu.VMEM((n_rows, sum(pieces_of(sizes, owned)), bw), F32),
            pltpu.VMEM((total, bw), F32),
            pltpu.VMEM((3, bw, bw), F32),
            pltpu.VMEM((3, bw, bw), F32),
            pltpu.VMEM((2, 2 * bw, 2 * bw), BF16),
            pltpu.VMEM((2, 2 * bw, 2 * bw), BF16),
            pltpu.VMEM((n, each, rows), F32),
            pltpu.VMEM((2, bw, max(early)), F32),
            pltpu.VMEM((n // 2, each, max(early)), F32),
            pltpu.VMEM((2, bw, ahead), F32),
            pltpu.VMEM((bw, 2 * bw), F32),
            pltpu.VMEM((bw, 2 * bw), F32),
            dma((nb,)), dma((nb,)), dma((nb,)), dma((nb,)),
            dma((3,)), dma((3,)), dma((3,)), dma((3,)),
            dma((3,)), dma((3,)), dma((2,)), dma((2, rows // step, 3)), dma((2,)), dma((2,)),
            dma, dma, dma((2,)), dma((2,)),
        ],
        compiler_params=pltpu.CompilerParams(
            collective_id=0, has_side_effects=True, vmem_limit_bytes=60 * 1024 * 1024
        ),
    )(observed, estimate, mask, threshold.reshape(1, width))
    landed = landed.reshape(n_rows, n_pairs, each, rows)
    return pl.pallas_call(
        interleave,
        out_shape=jax.ShapeDtypeStruct((each * n_pairs, n_rows * rows), F32),
        in_specs=[pl.BlockSpec(memory_space=pl.ANY)],
        out_specs=pl.BlockSpec(memory_space=pl.ANY),
        scratch_shapes=[
            pltpu.VMEM((n_rows, n_pairs, each, rows), F32),
            pltpu.VMEM((each * n_pairs, n_rows * rows), F32),
            dma((n_rows,)), dma((n_rows,)),
        ],
    )(landed)


def solution(mesh):
    placed = (P("rows", "pairs"), P("rows", "pairs"), P("rows", "pairs"), P("pairs"))
    return jax.shard_map(
        on_device, mesh=mesh, in_specs=placed, out_specs=P(("rows", "pairs"), None), check_vma=False
    )
```

```python
import functools

import jax
import jax.numpy as jnp
from jax import lax
from jax.experimental import pallas as pl
from jax.experimental.pallas import tpu as pltpu
from jax.sharding import PartitionSpec as P

MESH = pl.DeviceIdType.MESH
F32 = jnp.float32
BF16 = jnp.bfloat16
NN = (((1,), (0,)), ((), ()))
NT = (((1,), (1,)), ((), ()))


def split(a):
    high = a.astype(BF16)
    return high, (a - high.astype(F32)).astype(BF16)


def dot_parts(a, b, dims):
    def one(x, y):
        return lax.dot_general(x, y, dims, preferred_element_type=F32)

    return one(a[0], b[0]) + (one(a[0], b[1]) + one(a[1], b[0]))


def dot3(a, b, dims=NN):
    return dot_parts(split(a), split(b), dims)


def whitening_t(gram):
    width = gram.shape[0]
    eye = (
        lax.broadcasted_iota(jnp.int32, (width, width), 0)
        == lax.broadcasted_iota(jnp.int32, (width, width), 1)
    ).astype(F32)
    on_diag = gram * eye
    d_col = jnp.sum(on_diag, axis=1, keepdims=True) + 1e-06
    d_row = jnp.sum(on_diag, axis=0, keepdims=True) + 1e-06
    i_col = 1.0 / jnp.sqrt(d_col)
    i_row = 1.0 / jnp.sqrt(d_row)
    normed = gram * i_col * i_row
    sq = jnp.sum(jnp.sum(normed * normed, axis=0, keepdims=True), axis=1, keepdims=True)
    fro = jnp.sqrt(sq)
    y = normed / fro
    square_y = dot3(y, y)
    t = 1.5 * eye - 0.5 * y
    square_t = 2.25 * eye - 1.5 * y + 0.25 * square_y
    zy, zyt = dot3(y, square_t), dot3(1.5 * y - 0.5 * square_y, square_t)
    t_next = 1.5 * eye - 0.5 * zy
    z, tail, square_t = dot3(t, t_next), dot3(zyt, t_next), dot3(t_next, t_next)
    z = 1.5 * z - 0.5 * dot3(tail, square_t)
    return jnp.sqrt(d_col) * z * i_row / jnp.sqrt(fro)


def join(ss, sm, mm):
    top = jnp.concatenate([ss, sm], axis=1)
    low = jnp.concatenate([sm.T, mm], axis=1)
    return jnp.concatenate([top, low], axis=0)


def square(width):
    shape = (width, width)
    return lax.broadcasted_iota(jnp.int32, shape, 0), lax.broadcasted_iota(jnp.int32, shape, 1)


def pack(gram, n_own):
    bw = gram.shape[0] // 2
    ss, sm, mm = gram[:bw, :bw], gram[:bw, bw:], gram[bw:, bw:]
    r, c = square(bw)
    diag = jnp.sum(jnp.where(r == c, mm, 0.0), axis=0, keepdims=True)
    return [jnp.where(r <= c, ss, mm), sm, jnp.broadcast_to(diag, (8 * n_own, bw))]


def unpack(packed):
    bw = packed.shape[1]
    both, sm, diag = packed[:bw], packed[bw : 2 * bw], packed[2 * bw : 2 * bw + 1]
    r, c = square(bw)
    flip = both.T
    mm = jnp.where(r == c, diag, jnp.where(r > c, both, flip))
    return join(jnp.where(r <= c, both, flip), sm, mm)


def owners(n_rows):
    if n_rows % 4:
        return [(0, n_rows)] * 8
    return [(n_rows // 4, n_rows // 2)] * 8


def sizes_of(bw, n_own):
    return [2 * bw + 8 * n_own] * 2 + [bw] * 6


def pieces_of(sizes, owned):
    return [size // n_own for size, (_, n_own) in zip(sizes, owned)]


def kernel(
    n_rows, n_pairs, step, early, ahead,
    obs_ref, est_ref, mask_ref, thr_ref, out_ref,
    obs_in, est_in, mask_in, x, keep, pay, land, res, gmm_out, gmm_in, last_hi, last_lo, send, far, onward, raw, v_out, v_in,
    rs_s, rs_r, ag_s, ag_r, pm_s, pm_r, pg_s, pg_r, out_s, out_r, own_sem, in_sem, far_s, far_r,
    raw_s, raw_r, v_s, v_r,
):
    me = lax.axis_index("rows")
    group = lax.axis_index("pairs")
    n = n_rows * n_pairs
    bw = x.shape[2]
    rows = x.shape[3]
    chunks = rows // step
    each = send.shape[1]
    count = n // 2
    side = me // (n_rows // 2)
    partner = lax.rem(me + n_rows // 2, n_rows)
    partner_k = partner * n_pairs + group
    owned = owners(n_rows)
    sizes = sizes_of(bw, owned[0][1])

    def fetches(half, c):
        cols = pl.ds(half * 2 * bw, 2 * bw)
        part = pl.ds(c * step, step)
        pairs = ((obs_ref, obs_in), (est_ref, est_in), (mask_ref, mask_in))
        return [
            pltpu.make_async_copy(src.at[part, cols], dst.at[part, cols], in_sem.at[half, c, i])
            for i, (src, dst) in enumerate(pairs)
        ]

    def fetch_start(half):
        for c in range(chunks):
            for fetch in fetches(half, c):
                fetch.start()

    fetch_start(1)

    barrier = pltpu.get_barrier_semaphore()
    my_k = me * n_pairs + group

    def greet(i, carry):
        k = lax.rem(my_k + i, n)
        pl.semaphore_signal(
            barrier, inc=1, device_id=(k // n_pairs, lax.rem(k, n_pairs)), device_id_type=MESH
        )
        return carry

    lax.fori_loop(1, n, greet, 0)

    fetch_start(0)

    def fill_gram(half):
        total = jnp.zeros((2 * bw, 2 * bw), F32)
        for c in range(chunks):
            part = slice(c * step, (c + 1) * step)
            for fetch in fetches(half, c):
                fetch.wait()
            for slot in (2 * half, 2 * half + 1):
                cols = slice(slot * bw, (slot + 1) * bw)
                filled = jnp.where(mask_in[part, cols] == 1, obs_in[part, cols], est_in[part, cols])
                x[0, slot, :, part] = filled.T
            both = split(jnp.concatenate([x[0, 2 * half, :, part], x[0, 2 * half + 1, :, part]], axis=0))
            total += dot_parts(both, both, NT)
        return total

    def cross_gram(s, m):
        total = jnp.zeros((2 * bw, 2 * bw), F32)
        for c in range(chunks):
            part = slice(c * step, (c + 1) * step)
            s_parts = jnp.concatenate(split(s[:, part]), axis=0)
            m_parts = jnp.concatenate(split(m[:, part]), axis=0)
            total += lax.dot_general(s_parts, m_parts, NT, preferred_element_type=F32)
        return total[:bw, :bw] + (total[:bw, bw:] + total[bw:, :bw])

    def place(b):
        pieces = pieces_of(sizes, owned)
        return sum(sizes[:b]), sum(pieces[:b]), pieces[b]

    def owner(b):
        first, n_own = owned[b]
        return (me >= first) & (me < first + n_own)

    def own(b, q):
        base, _, piece = place(b)
        return pl.ds(pl.multiple_of(base + q * piece, 8), piece)

    def fill_pay(b, blocks):
        at = place(b)[0]
        for block in blocks:
            pay[at : at + block.shape[0], :] = block
            at += block.shape[0]

    def reduce_start(b, blocks=()):
        _, lbase, piece = place(b)
        first, n_own = owned[b]
        fill_pay(b, blocks)
        if b == 0:
            pl.semaphore_wait(barrier, n - 1)

        def scatter(i, carry):
            q = lax.rem(me + i, n_own)
            peer = first + q

            @pl.when(peer != me)
            def _():
                pltpu.make_async_remote_copy(
                    pay.at[own(b, q)], land.at[lax.rem(me + n_rows - peer, n_rows), pl.ds(lbase, piece)],
                    rs_s.at[b], rs_r.at[b], device_id=(peer, group), device_id_type=MESH,
                ).start()

            return carry

        lax.fori_loop(0, n_own, scatter, 0)

    def wait_pieces(b, some, sem):
        _, lbase, piece = place(b)
        ref = land.at[pl.ds(0, some), pl.ds(lbase, piece)]
        pltpu.make_async_copy(ref, ref, sem).wait()

    def reduce_mid(b):
        _, lbase, piece = place(b)

        @pl.when(owner(b))
        def _():
            wait_pieces(b, n_rows - 1, rs_r.at[b])
            mine = own(b, me - owned[b][0])
            total = pay[mine, :]
            for off in range(1, n_rows):
                total += land[off, lbase : lbase + piece, :]
            res[mine, :] = total

            def gather(off, carry):
                peer = lax.rem(me + off, n_rows)
                pltpu.make_async_remote_copy(
                    res.at[mine], res.at[mine],
                    ag_s.at[b], ag_r.at[b], device_id=(peer, group), device_id_type=MESH,
                ).start()
                return carry

            lax.fori_loop(1, n_rows, gather, 0)

    def pieces_to_owners(b, sem):
        @pl.when(owner(b))
        def _():
            if owned[b][1] > 1:
                wait_pieces(b, owned[b][1] - 1, sem)

        @pl.when(jnp.logical_not(owner(b)))
        def _():
            wait_pieces(b, owned[b][1], sem)

    def reduce_end(b):
        base, _, _ = place(b)
        pieces_to_owners(b, ag_r.at[b])
        return res[base : base + sizes[b], :]

    def settle(b):
        pieces_to_owners(b, rs_s.at[b])

        @pl.when(owner(b))
        def _():
            wait_pieces(b, n_rows - 1, ag_s.at[b])

    def put(v_parts, s, m, write, start=0, stop=None):
        stop = s.shape[1] if stop is None else stop
        for at in range(start, stop, step):
            part = slice(at, min(at + step, stop))
            both = split(jnp.concatenate([s[:, part], m[:, part]], axis=0))
            write(part, dot_parts(v_parts, both, NN))

    def into(ref):
        def write(part, value):
            ref[:, part] = value
        return write

    right = lax.rem(group + 1, n_pairs)

    def pass_copy(src, dst, send_sem, recv_sem):
        return pltpu.make_async_remote_copy(
            src, dst, send_sem, recv_sem, device_id=(me, right), device_id_type=MESH
        )

    skip = (ahead, 0, 0)

    def put_and_pass(i, v_half, s, m):
        def write(part, value):
            keep[i, :, part] = value
            pass_copy(
                keep.at[i, :, part], x.at[i + 1, 1, :, part], pm_s.at[i], pm_r.at[i]
            ).start()

        put(split(v_half), s, m, write, skip[i])

    def pass_gram(i, gmm):
        gmm_out[i] = gmm
        small = pass_copy(gmm_out.at[i], gmm_in.at[i], pg_s.at[i], pg_r.at[i])
        small.start()
        main = pass_copy(
            keep.at[i, :, skip[i] :], x.at[i + 1, 1, :, skip[i] :], pm_s.at[i], pm_r.at[i]
        )
        return main, small

    raw_copy = pass_copy(x.at[0, 2:4, :, :ahead], raw, raw_s, raw_r)
    odd = lax.rem(me, 2)
    sibling = me + 1 - 2 * odd
    mine_v = pl.ds(pl.multiple_of(odd * (bw // 2), 8), bw // 2)
    other_v = pl.ds(pl.multiple_of((1 - odd) * (bw // 2), 8), bw // 2)
    v_pass = pass_copy(v_out.at[mine_v], v_in.at[mine_v], v_s.at[0], v_r.at[0])
    v_share = pltpu.make_async_remote_copy(
        v_in.at[mine_v], v_in.at[mine_v], v_s.at[1], v_r.at[1],
        device_id=(sibling, group), device_id_type=MESH,
    )
    v_shared = pltpu.make_async_remote_copy(
        v_in.at[other_v], v_in.at[other_v], v_s.at[1], v_r.at[1],
        device_id=(sibling, group), device_id_type=MESH,
    )

    def new_grams(v, gram):
        vg = dot3(v, gram)
        return dot3(vg[:bw], v[:bw], NT), dot3(vg[bw:], v[bw:], NT)

    def far_copy(half, j, at, size):
        return pltpu.make_async_remote_copy(
            x.at[3, 2 * half + j, :, pl.ds(at, size)], far.at[j, :, pl.ds(at, size)],
            far_s.at[j], far_r.at[j], device_id=(partner, group), device_id_type=MESH,
        )

    shipped = [0, 0]

    def ship(half, some):
        n_early = early[half] // 128
        upto = min(shipped[half] + some, 2 * n_early)

        @pl.when(side != half)
        def _():
            for i in range(shipped[half], upto):
                far_copy(half, i // n_early, i % n_early * 128, 128).start()

        shipped[half] = upto

    def scale_last(half, v, gram):
        vg = dot3(v, gram)
        squares = jnp.sum(vg * v, axis=1, keepdims=True)
        norm = jnp.sqrt(squares + 1e-06)
        eye = (
            lax.broadcasted_iota(jnp.int32, gram.shape, 0)
            == lax.broadcasted_iota(jnp.int32, gram.shape, 1)
        )
        level = thr_ref[:, 2 * half * bw : 2 * (half + 1) * bw]
        level = jnp.sum(jnp.where(eye, level, 0.0), axis=1, keepdims=True)
        last_hi[half], last_lo[half] = split((jnp.maximum(norm - level, 0.0) / norm) * v)

    per_block = bw // each

    def finish(half, target, base, s, m, start, stop, slots=(0, 1)):
        for j in slots:
            def write(part, value):
                for i in range(per_block):
                    target[base + j * per_block + i, :, part] = value[i * each : (i + 1) * each]

            cut = slice(j * bw, (j + 1) * bw)
            put((last_hi[half, cut], last_lo[half, cut]), s, m, write, start, stop)

    def to(k):
        return dict(device_id=(k // n_pairs, lax.rem(k, n_pairs)), device_id_type=MESH)

    def deliver(half, same, begin=0, some=count):
        def go(i, carry):
            k = half * count + begin + lax.rem(my_k + i, some)
            if not same:
                pltpu.make_async_remote_copy(
                    send.at[k, :, early[half] :], out_ref.at[my_k, :, early[half] :],
                    out_s.at[1], out_r.at[1], **to(k)
                ).start()
                return carry

            @pl.when(k != my_k)
            def _():
                pltpu.make_async_remote_copy(
                    send.at[k], out_ref.at[my_k], out_s.at[0], out_r.at[0], **to(k)
                ).start()

            @pl.when(k == my_k)
            def _():
                pltpu.make_async_copy(send.at[k], out_ref.at[my_k], own_sem.at[0]).start()

            return carry

        lax.fori_loop(0, some, go, 0)

    def deliver_onward(half):
        def go(i, carry):
            at = lax.rem(my_k + i, count)
            k = half * count + at
            some = onward.at[at, :, : early[half]]
            spot = out_ref.at[partner_k, :, : early[half]]

            @pl.when(k != my_k)
            def _():
                pltpu.make_async_remote_copy(
                    some, spot, out_s.at[2], out_r.at[2], **to(k)
                ).start()

            @pl.when(k == my_k)
            def _():
                pltpu.make_async_copy(some, spot, own_sem.at[1]).start()

            return carry

        lax.fori_loop(0, count, go, 0)

    def compute_last(half):
        s, m = x.at[3, 2 * half], x.at[3, 2 * half + 1]
        finish(half, send, half * count, s, m, early[half], rows)

        @pl.when(side == half)
        def _():
            finish(half, send, half * count, s, m, 0, early[half])

    def deliver_other(half):
        @pl.when(side != half)
        def _():
            deliver(half, False)

    def deliver_own(half):
        @pl.when(side == half)
        def _():
            deliver(half, True)

    reduce_start(0, pack(fill_gram(1), owned[0][1]))
    raw_copy.start()
    fill_pay(1, pack(fill_gram(0), owned[1][1]))
    reduce_start(1)
    reduce_mid(0)
    reduce_mid(1)
    gb = unpack(reduce_end(0))
    vb = whitening_t(gb)
    v_out[...] = vb[bw:]
    v_pass.start()
    put_and_pass(0, vb[bw:], x.at[0, 2], x.at[0, 3])
    bs, bm = new_grams(vb, gb)
    sent = [pass_gram(0, bm)]
    put(split(vb[:bw]), x.at[0, 2], x.at[0, 3], into(x.at[1, 2]))
    ga = unpack(reduce_end(1))
    va = whitening_t(ga)
    put(split(va[bw:]), x.at[0, 0], x.at[0, 1], into(x.at[1, 3]))

    reduce_start(2, [cross_gram(x.at[1, 2], x.at[1, 3])])
    put(split(va[:bw]), x.at[0, 0], x.at[0, 1], into(x.at[1, 0]))
    v_pass.wait_recv()
    v_share.start()
    as_, am = new_grams(va, ga)
    reduce_mid(2)
    gb = join(bs, reduce_end(2), am)
    vb = whitening_t(gb)
    put_and_pass(1, vb[bw:], x.at[1, 2], x.at[1, 3])
    raw_copy.wait_recv()
    v_shared.wait_recv()
    put(split(v_in[...]), raw.at[0], raw.at[1], into(x.at[1, 1]))
    for c in sent[0]:
        c.wait_recv()
    reduce_start(3, [cross_gram(x.at[1, 0], x.at[1, 1])])
    bs, bm = new_grams(vb, gb)
    sent.append(pass_gram(1, bm))
    put(split(vb[:bw]), x.at[1, 2], x.at[1, 3], into(x.at[2, 2]))
    reduce_mid(3)
    ga = join(as_, reduce_end(3), gmm_in[0])
    va = whitening_t(ga)
    put(split(va[bw:]), x.at[1, 0], x.at[1, 1], into(x.at[2, 3]))

    reduce_start(4, [cross_gram(x.at[2, 2], x.at[2, 3])])
    put(split(va[:bw]), x.at[1, 0], x.at[1, 1], into(x.at[2, 0]))
    as_, am = new_grams(va, ga)
    reduce_mid(4)
    gb = join(bs, reduce_end(4), am)
    vb = whitening_t(gb)
    put_and_pass(2, vb[bw:], x.at[2, 2], x.at[2, 3])
    for c in sent[1]:
        c.wait_recv()
    reduce_start(5, [cross_gram(x.at[2, 0], x.at[2, 1])])
    bs, bm = new_grams(vb, gb)
    sent.append(pass_gram(2, bm))
    put(split(vb[:bw]), x.at[2, 2], x.at[2, 3], into(x.at[3, 2]))
    ship(1, SHIP[0])
    reduce_mid(5)
    ship(1, SHIP[1])
    ga = join(as_, reduce_end(5), gmm_in[1])
    va = whitening_t(ga)
    put(split(va[bw:]), x.at[2, 0], x.at[2, 1], into(x.at[3, 3]))

    reduce_start(6, [cross_gram(x.at[3, 2], x.at[3, 3])])
    ship(1, SHIP[2])
    put(split(va[:bw]), x.at[2, 0], x.at[2, 1], into(x.at[3, 0]))
    ship(0, SHIP[3])
    as_, am = new_grams(va, ga)
    reduce_mid(6)
    ship(1, SHIP[4])
    ship(0, min(SHIP[5], early[0] // 128 - SHIP[3]))
    for c in sent[2]:
        c.wait_recv()
    reduce_start(7, [cross_gram(x.at[3, 0], x.at[3, 1])])
    ship(1, SHIP[6])
    ship(0, SHIP[7])
    gb = join(bs, reduce_end(6), am)
    scale_last(1, whitening_t(gb), gb)
    compute_last(1)
    reduce_mid(7)
    ship(1, 2 * early[1] // 128)
    ship(0, 2 * early[0] // 128)
    ga = join(as_, reduce_end(7), gmm_in[2])
    deliver_other(1)
    deliver_own(1)
    scale_last(0, whitening_t(ga), ga)
    for j in range(2):
        finish(0, send, 0, x.at[3, 0], x.at[3, 1], early[0], rows, (j,))

        @pl.when(side != 0)
        def _():
            deliver(0, False, j * per_block, per_block)

        @pl.when(side == 0)
        def _():
            finish(0, send, 0, x.at[3, 0], x.at[3, 1], 0, early[0], (j,))
            deliver(0, True, j * per_block, per_block)

    for half in (1, 0):
        @pl.when(side == half)
        def _():
            for j in range(2):
                far_copy(half, j, 0, early[half]).wait_recv()
            finish(half, onward, 0, far.at[0], far.at[1], 0, early[half])
            deliver_onward(half)

    for b in range(len(sizes)):
        settle(b)
    for pair in sent:
        for c in pair:
            c.wait_send()
    raw_copy.wait_send()
    v_pass.wait_send()
    v_share.wait_send()
    pltpu.make_async_copy(send.at[0], out_ref.at[my_k], own_sem.at[0]).wait()

    def done(ref, sem):
        pltpu.make_async_copy(ref, ref, sem).wait()

    for half in (0, 1):
        @pl.when(side == half)
        def _():
            for j in range(2):
                far_copy(1 - half, j, 0, early[1 - half]).wait_send()
            done(onward.at[0, :, : early[half]], own_sem.at[1])
            done(send.at[pl.ds(0, count - 1)], out_s.at[0])
            done(send.at[pl.ds(0, count), :, early[1 - half] :], out_s.at[1])
            done(onward.at[pl.ds(0, count - 1), :, : early[half]], out_s.at[2])
            done(out_ref.at[pl.ds(0, count - 1)], out_r.at[0])
            done(out_ref.at[pl.ds(0, count), :, early[half] :], out_r.at[1])
            done(out_ref.at[pl.ds(0, count - 1), :, : early[half]], out_r.at[2])


def interleave(in_ref, out_ref, taken, mixed, in_sem, out_sem):
    n_rows, n_pairs, each, rows = in_ref.shape
    ins = [pltpu.make_async_copy(in_ref.at[r], taken.at[r], in_sem.at[r]) for r in range(n_rows)]
    for copy in ins:
        copy.start()
    outs = []
    for r in range(n_rows):
        cols = slice(r * rows, (r + 1) * rows)
        ins[r].wait()
        for i in range(each):
            mixed[i * n_pairs : (i + 1) * n_pairs, cols] = taken[r, :, i, :]
        outs.append(pltpu.make_async_copy(mixed.at[:, cols], out_ref.at[:, cols], out_sem.at[r]))
        outs[-1].start()
    for copy in outs:
        copy.wait()


EARLY = (4, 4)
SHIP = (1, 1, 2, 1, 1, 2, 1, 1)


def on_device(observed, estimate, mask, threshold):
    n_rows = lax.axis_size("rows")
    n_pairs = lax.axis_size("pairs")
    rows, width = observed.shape
    bw = width // 4
    n = n_rows * n_pairs
    each = width // n
    step = 512 if rows % 512 == 0 else rows
    early = [rows * part // 12 // 128 * 128 or rows for part in EARLY]
    ahead = rows * 5 // 12 // 128 * 128 or rows
    owned = owners(n_rows)
    sizes = sizes_of(bw, owned[0][1])
    total = sum(sizes)
    vmem = pl.BlockSpec(memory_space=pltpu.VMEM)
    dma = pltpu.SemaphoreType.DMA
    nb = len(sizes)
    landed = pl.pallas_call(
        functools.partial(kernel, n_rows, n_pairs, step, early, ahead),
        out_shape=jax.ShapeDtypeStruct((n, each, rows), F32),
        in_specs=[pl.BlockSpec(memory_space=pl.ANY)] * 3 + [vmem],
        out_specs=pl.BlockSpec(memory_space=pl.ANY),
        scratch_shapes=[
            pltpu.VMEM((rows, width), F32),
            pltpu.VMEM((rows, width), F32),
            pltpu.VMEM((rows, width), jnp.int32),
            pltpu.VMEM((4, 4, bw, rows), F32),
            pltpu.VMEM((3, bw, rows), F32),
            pltpu.VMEM((total, bw), F32),
            pltpu.VMEM((n_rows, sum(pieces_of(sizes, owned)), bw), F32),
            pltpu.VMEM((total, bw), F32),
            pltpu.VMEM((3, bw, bw), F32),
            pltpu.VMEM((3, bw, bw), F32),
            pltpu.VMEM((2, 2 * bw, 2 * bw), BF16),
            pltpu.VMEM((2, 2 * bw, 2 * bw), BF16),
            pltpu.VMEM((n, each, rows), F32),
            pltpu.VMEM((2, bw, max(early)), F32),
            pltpu.VMEM((n // 2, each, max(early)), F32),
            pltpu.VMEM((2, bw, ahead), F32),
            pltpu.VMEM((bw, 2 * bw), F32),
            pltpu.VMEM((bw, 2 * bw), F32),
            dma((nb,)), dma((nb,)), dma((nb,)), dma((nb,)),
            dma((3,)), dma((3,)), dma((3,)), dma((3,)),
            dma((3,)), dma((3,)), dma((2,)), dma((2, rows // step, 3)), dma((2,)), dma((2,)),
            dma, dma, dma((2,)), dma((2,)),
        ],
        compiler_params=pltpu.CompilerParams(
            collective_id=0, has_side_effects=True, vmem_limit_bytes=60 * 1024 * 1024
        ),
    )(observed, estimate, mask, threshold.reshape(1, width))
    landed = landed.reshape(n_rows, n_pairs, each, rows)
    return pl.pallas_call(
        interleave,
        out_shape=jax.ShapeDtypeStruct((each * n_pairs, n_rows * rows), F32),
        in_specs=[pl.BlockSpec(memory_space=pl.ANY)],
        out_specs=pl.BlockSpec(memory_space=pl.ANY),
        scratch_shapes=[
            pltpu.VMEM((n_rows, n_pairs, each, rows), F32),
            pltpu.VMEM((each * n_pairs, n_rows * rows), F32),
            dma((n_rows,)), dma((n_rows,)),
        ],
    )(landed)


def solution(mesh):
    placed = (P("rows", "pairs"), P("rows", "pairs"), P("rows", "pairs"), P("pairs"))
    return jax.shard_map(
        on_device, mesh=mesh, in_specs=placed, out_specs=P(("rows", "pairs"), None), check_vma=False
    )
```
